32 devices in a mesh: tile: 8 (over y, x, core), chan: 4 (over z).
Axes of the slice: x: 2, y: 2, z: 4, core: 2. Of those that a mesh axis runs over, the one named last changes fastest.
Arguments:
- ensemble: bfloat16 [3072, 128, 256], P('tile', 'chan'), may hold values from -6 to 6
- jacobian: bfloat16 [1280, 128, 128], P('tile', 'chan'), may hold values from -1 to 1
- innovation: float32 [1280, 128], P('tile', 'chan'), may hold values from -6 to 6
- error_vectors: float32 [128, 32], replicated, may hold values from -1 to 1, as said below
- error_values: float32 [128], replicated, may hold values from 0.25 to 4
- ensemble_vectors: float32 [256, 256], replicated, may hold values from -1 to 1, as said below
- column_pick: int32 [8, 5, 40], P('tile'), may hold values from 0 to 383
- footprint_slot: int32 [1280], P('tile'), may hold values from 0 to 199, as said below
- footprint_count: int32 [8], P('tile'), may hold values from 20 to 160, as said below
Outputs:
- analysis: bfloat16 [3072, 128, 256], P('tile', 'chan')
The draws below stay inside these ranges and needn't reach their ends.
Inputs may be any that keep to these rules, and one draw needn't show every extreme that they name: `footprint_slot`: the 160 entries of one pack are distinct; slot o * 40 + j is the j-th column that tile (pack + 2 - o) mod 8 sends to this pack. `footprint_count`: some pack has all 160 footprints live. `error_vectors`: each block of 32 rows is an orthogonal matrix. `ensemble_vectors`: an orthogonal matrix.
All inputs are finite; a program needn't handle non-finite values.
Results may differ from the reference program's by a relative error of at most 0.013.
Values may be sent and summed in bfloat16 or wider, within the bound.
A program may use at most 64 MiB of HBM per device.

```python
import math
import jax
import jax.numpy as jnp
from jax import lax

ENS = 256
LEV = 128
CH_DEV = 32
REACH = 2
F_DEV = 160
COLS_DEV = 384
SPAN = 5
CAP = 40
CHANNELS = 128
PACKS = 8
FOOTPRINTS = 1280
COLUMNS = 3072


def draw_error_vectors(key, part):
    blocks = jax.random.normal(key, (CHANNELS // CH_DEV, CH_DEV, CH_DEV), jnp.float32)
    basis_blocks = jnp.linalg.qr(blocks)[0]
    return basis_blocks.reshape(CHANNELS, CH_DEV).astype(jnp.float32)


def draw_ensemble_vectors(key, part):
    square = jax.random.normal(key, (ENS, ENS), jnp.float32)
    return jnp.linalg.qr(square)[0].astype(jnp.float32)


def draw_footprint_slot(key, part):
    pack_keys = jax.random.split(jax.random.fold_in(key, 11), PACKS)
    orders = jax.vmap(lambda single: jax.random.permutation(single, SPAN * CAP))(pack_keys)
    return orders[:, :F_DEV].reshape(-1).astype(jnp.int32)


def draw_footprint_count(key, part):
    base_counts = jax.random.randint(jax.random.fold_in(key, 23), (PACKS,), F_DEV // 8, F_DEV // 2 + 1)
    busiest = jax.random.randint(jax.random.fold_in(key, 29), (), 0, PACKS)
    return jnp.where(jnp.arange(PACKS) == busiest, F_DEV, base_counts).astype(jnp.int32)


def smooth_levels(sub_key, leading):
    raw = jax.random.normal(sub_key, leading + (LEV + 15,), jnp.float32)
    summed = jnp.concatenate([jnp.zeros(leading + (1,), jnp.float32), jnp.cumsum(raw, axis=-1)], axis=-1)
    return (summed[..., 16:] - summed[..., :-16]) / 4.0


def draw_jacobian(key, part):
    sigma = (1000.0 / (LEV * FOOTPRINTS * CHANNELS)) ** 0.5
    limit = min(6.0 * sigma, 1.0)
    block_count = FOOTPRINTS // F_DEV

    def one_block(index):
        sub_keys = jax.random.split(jax.random.fold_in(jax.random.fold_in(key, 101), index), 4)
        level_common = jax.random.normal(sub_keys[0], (F_DEV, 1, 1), jnp.float32)
        profile = 0.8 * level_common + 0.6 * smooth_levels(sub_keys[1], (F_DEV, 1))
        channel_part = smooth_levels(sub_keys[2], (F_DEV, CHANNELS))
        white = jax.random.normal(sub_keys[3], (F_DEV, CHANNELS, LEV), jnp.float32)
        values = 0.8 * profile + 0.4 * channel_part + 0.45 * white
        return jnp.clip(values * sigma, -limit, limit)
    blocks = lax.map(one_block, jnp.arange(block_count, dtype=jnp.int32))
    return blocks.reshape(FOOTPRINTS, CHANNELS, LEV).astype(jnp.bfloat16)


def place_ends(array, key, smallest, high):
    dims = array.shape
    spot = [jax.random.randint(jax.random.fold_in(key, axis), (), 0, dims[axis]) for axis in range(len(dims))]
    array = array.at[tuple(spot)].set(smallest)
    longest = dims.index(max(dims))
    spot[longest] = (spot[longest] + 1) % dims[longest]
    return array.at[tuple(spot)].set(high)


def block_levels(stream_key, extent, pieces, least, high):
    factor_of = 1.0
    for dim, parts in pieces:
        draws = jax.random.uniform(jax.random.fold_in(jax.random.fold_in(stream_key, 6), dim), (parts,), jnp.float32, least / len(pieces), high / len(pieces))
        factor_of = factor_of * jnp.repeat(jnp.exp(draws), extent[dim] // parts).reshape((-1,) + (1,) * (len(extent) - 1 - dim))
    return factor_of


def scatter_about(rng, extent, scale, bound, shards=(), kind=jnp.bfloat16):
    array = scale * jax.random.normal(rng, extent, jnp.float32)
    if shards:
        array = array * block_levels(rng, extent, shards, -0.22, 0.18)
    return jnp.clip(array, -bound, bound).astype(kind)


def setup_inputs(seed: int = 0) -> dict:
    splits = jax.random.split(jax.random.key(seed), 10)
    return {
        "ensemble": scatter_about(splits[0], (COLUMNS, LEV, ENS), 1.0, 6.0, ((0, 8), (1, 4))),
        "jacobian": draw_jacobian(jax.random.fold_in(splits[9], 71), 0),
        "innovation": scatter_about(splits[2], (FOOTPRINTS, CHANNELS), 1.0, 6.0, ((0, 8), (1, 4)), jnp.float32),
        "error_vectors": draw_error_vectors(jax.random.fold_in(splits[9], 71), 0),
        "error_values": jnp.clip(jnp.exp(jax.random.uniform(splits[4], (CHANNELS,), jnp.float32, math.log(0.25), math.log(4.0))), 0.25, 4.0),
        "ensemble_vectors": draw_ensemble_vectors(jax.random.fold_in(splits[9], 71), 0),
        "column_pick": place_ends(jax.random.randint(splits[6], (PACKS, SPAN, CAP), 0, COLS_DEV), jax.random.fold_in(splits[6], 1), 0, COLS_DEV - 1).astype(jnp.int32),
        "footprint_slot": draw_footprint_slot(jax.random.fold_in(splits[9], 71), 0),
        "footprint_count": draw_footprint_count(jax.random.fold_in(splits[9], 71), 0),
    }


def turn_blocks(values, vectors):
    row_count, channels, members = values.shape
    group_width = vectors.shape[1]
    grouped = values.reshape(row_count, channels // group_width, group_width, members)
    basis_blocks = vectors.reshape(channels // group_width, group_width, group_width)
    turned = jnp.einsum('gce,fgck->fgek', basis_blocks, grouped, precision=lax.Precision.HIGHEST)
    return turned.reshape(row_count, channels, members)

def turn_rows(values, vectors):
    row_count, channels = values.shape
    group_width = vectors.shape[1]
    grouped = values.reshape(row_count, channels // group_width, group_width)
    basis_blocks = vectors.reshape(channels // group_width, group_width, group_width)
    turned = jnp.einsum('gce,fgc->fge', basis_blocks, grouped, precision=lax.Precision.HIGHEST)
    return turned.reshape(row_count, channels)

def reference(ensemble, jacobian, innovation, error_vectors, error_values, ensemble_vectors, column_pick, footprint_slot, footprint_count):
    members = ensemble.shape[2]
    scales = 1.0 / jnp.sqrt(error_values)

    def pack_terms(carried, pack_index):
        gram_sum, pull_sum = carried
        slot_ids = lax.dynamic_slice_in_dim(footprint_slot, pack_index * F_DEV, F_DEV, 0)
        offset = slot_ids // CAP
        place_ids = slot_ids % CAP
        source = (pack_index + REACH - offset) % PACKS
        local_ids = column_pick[source, offset, place_ids]
        columns = jnp.take(ensemble, (source * COLS_DEV + local_ids).astype(jnp.int32), axis=0)
        sensitivity = lax.dynamic_slice_in_dim(jacobian, pack_index * F_DEV, F_DEV, 0)
        response = jnp.einsum('fcl,flk->fck', sensitivity.astype(jnp.float32), columns.astype(jnp.float32), precision=lax.Precision.HIGHEST)
        live_rows = (jnp.arange(F_DEV, dtype=jnp.int32) < footprint_count[pack_index]).astype(jnp.float32)
        whitened = turn_blocks(response, error_vectors) * scales[None, :, None] * live_rows[:, None, None]
        misfit_rows = lax.dynamic_slice_in_dim(innovation, pack_index * F_DEV, F_DEV, 0)
        misfit = turn_rows(misfit_rows, error_vectors) * scales[None, :]
        pull_sum = pull_sum + jnp.einsum('fck,fc->k', whitened, misfit, precision=lax.Precision.HIGHEST)
        rounded = whitened.astype(jnp.bfloat16).reshape(-1, members)
        gram_sum = gram_sum + lax.dot_general(rounded.astype(jnp.float32), rounded.astype(jnp.float32), (((0,), (0,)), ((), ())), preferred_element_type=jnp.float32)
        return ((gram_sum, pull_sum), None)
    initial = (jnp.zeros((members, members), jnp.float32), jnp.zeros((members,), jnp.float32))
    (gram_sum, pull_sum), _ = lax.scan(pack_terms, initial, jnp.arange(PACKS, dtype=jnp.int32))
    system = gram_sum + (members - 1) * jnp.eye(members, dtype=jnp.float32)
    factor = jnp.linalg.cholesky(system)
    halfway = lax.linalg.triangular_solve(factor, pull_sum[:, None], left_side=True, lower=True)
    mean_weights = lax.linalg.triangular_solve(factor, halfway, left_side=True, lower=True, transpose_a=True)[:, 0]
    spread = jnp.sqrt(members - 1.0) * lax.linalg.triangular_solve(factor, ensemble_vectors, left_side=True, lower=True, transpose_a=True)
    transform = (spread + mean_weights[:, None]).astype(jnp.bfloat16)
    blocks = ensemble.reshape(PACKS, COLS_DEV * LEV, members)

    def update(block):
        return jnp.dot(block.astype(jnp.float32), transform.astype(jnp.float32), preferred_element_type=jnp.float32).astype(jnp.bfloat16)
    return lax.map(update, blocks).reshape(COLUMNS, LEV, members)
```

```python
import functools
import jax
import jax.numpy as jnp
from jax import lax
from jax.experimental import pallas as pl
from jax.experimental.pallas import tpu as pltpu
from jax.sharding import PartitionSpec as P

MESH = pl.DeviceIdType.MESH


def greet(axes):
    barrier = pltpu.get_barrier_semaphore()
    total = 0
    for axis in axes:
        count = lax.axis_size(axis)
        here = lax.axis_index(axis)
        for step in range(1, count):
            pl.semaphore_signal(
                barrier, inc=1, device_id={axis: lax.rem(here + step, count)}, device_id_type=MESH
            )
        total += count - 1
    pl.semaphore_wait(barrier, total)


def sum_kernel(piece, x_ref, out_ref, landed, crossed, mine, summed, spread, sems_a, sems_b, sems_c):
    tiles = lax.axis_size("tile")
    chans = lax.axis_size("chan")
    tile = lax.axis_index("tile")
    chan = lax.axis_index("chan")
    greet(("tile", "chan"))

    def rows_of(index):
        return pl.ds(pl.multiple_of(index * piece, 8), piece)

    copies = []
    for step in range(1, tiles):
        peer = lax.rem(tile + step, tiles)
        copies.append(
            pltpu.make_async_remote_copy(
                src_ref=x_ref.at[rows_of(peer)],
                dst_ref=landed.at[step],
                send_sem=sems_a.at[0, step],
                recv_sem=sems_a.at[1, step],
                device_id={"tile": peer},
                device_id_type=MESH,
            )
        )
    for copy in copies:
        copy.start()
    total = x_ref[rows_of(tile), :]
    for step, copy in enumerate(copies, 1):
        copy.wait_recv()
        total = total + landed[step]
    mine[...] = total
    crossings = []
    for step in range(1, chans):
        crossings.append(
            pltpu.make_async_remote_copy(
                src_ref=mine,
                dst_ref=crossed.at[step],
                send_sem=sems_b.at[0, step],
                recv_sem=sems_b.at[1, step],
                device_id={"chan": lax.rem(chan + step, chans)},
                device_id_type=MESH,
            )
        )
    for copy in crossings:
        copy.start()
    for step, copy in enumerate(crossings, 1):
        copy.wait_recv()
        total = total + crossed[step]
    summed[...] = total
    shares = []
    for step in range(1, tiles):
        shares.append(
            pltpu.make_async_remote_copy(
                src_ref=summed,
                dst_ref=spread.at[step],
                send_sem=sems_c.at[0, step],
                recv_sem=sems_c.at[1, step],
                device_id={"tile": lax.rem(tile + step, tiles)},
                device_id_type=MESH,
            )
        )
    for copy in shares:
        copy.start()
    out_ref[rows_of(tile), :] = total
    for step, copy in enumerate(shares, 1):
        copy.wait_recv()
        out_ref[rows_of(lax.rem(tile - step + tiles, tiles)), :] = spread[step]
    for copy in copies + crossings + shares:
        copy.wait_send()


def sum_all(gram, pull):
    tiles = lax.axis_size("tile")
    chans = lax.axis_size("chan")
    members = gram.shape[0]
    half = members // 2
    used = 3 * half + 8
    piece = -(-used // (8 * tiles)) * 8
    flat = jnp.concatenate(
        [
            gram[:half, :half],
            gram[:half, half:],
            gram[half:, half:],
            pull.reshape(2, half),
            jnp.zeros((piece * tiles - 3 * half - 2, half), jnp.float32),
        ],
        0,
    )
    out = pl.pallas_call(
        functools.partial(sum_kernel, piece),
        out_shape=jax.ShapeDtypeStruct(flat.shape, jnp.float32),
        in_specs=[pl.BlockSpec(memory_space=pltpu.VMEM)],
        out_specs=pl.BlockSpec(memory_space=pltpu.VMEM),
        scratch_shapes=[
            pltpu.VMEM((tiles, piece, half), jnp.float32),
            pltpu.VMEM((chans, piece, half), jnp.float32),
            pltpu.VMEM((piece, half), jnp.float32),
            pltpu.VMEM((piece, half), jnp.float32),
            pltpu.VMEM((tiles, piece, half), jnp.float32),
            pltpu.SemaphoreType.DMA((2, tiles)),
            pltpu.SemaphoreType.DMA((2, chans)),
            pltpu.SemaphoreType.DMA((2, tiles)),
        ],
        compiler_params=pltpu.CompilerParams(collective_id=0, has_side_effects=True),
        name="sum_all",
    )(flat)
    top = out[:half]
    across = out[half : 2 * half]
    low = out[2 * half : 3 * half]
    gram = jnp.concatenate(
        [jnp.concatenate([top, across], 1), jnp.concatenate([across.T, low], 1)], 0
    )
    return gram, out[3 * half : 3 * half + 2].reshape(members)


def apply_kernel(x_ref, w_ref, o_ref):
    o_ref[...] = jnp.dot(x_ref[...], w_ref[...], preferred_element_type=jnp.float32).astype(o_ref.dtype)


def apply_transform(rows, transform):
    count, members = rows.shape
    block = min(count, 2048)
    while count % block:
        block //= 2
    return pl.pallas_call(
        apply_kernel,
        grid=(count // block,),
        out_shape=jax.ShapeDtypeStruct(rows.shape, rows.dtype),
        in_specs=[
            pl.BlockSpec((block, members), lambda i: (i, 0)),
            pl.BlockSpec((members, members), lambda i: (0, 0)),
        ],
        out_specs=pl.BlockSpec((block, members), lambda i: (i, 0)),
        name="apply_transform",
    )(rows, transform)


def from_behind(value, axis, steps):
    count = lax.axis_size(axis)
    pairs = [(source, (source + steps) % count) for source in range(count)]
    return lax.ppermute(value, axis, pairs)


def turn_blocks(values, vectors):
    row_count, channels, members = values.shape
    group_width = vectors.shape[1]
    grouped = values.reshape(row_count, channels // group_width, group_width, members)
    basis_blocks = vectors.reshape(channels // group_width, group_width, group_width)
    turned = jnp.einsum("gce,fgck->fgek", basis_blocks, grouped, precision=lax.Precision.HIGHEST)
    return turned.reshape(row_count, channels, members)


def turn_rows(values, vectors):
    row_count, channels = values.shape
    group_width = vectors.shape[1]
    grouped = values.reshape(row_count, channels // group_width, group_width)
    basis_blocks = vectors.reshape(channels // group_width, group_width, group_width)
    turned = jnp.einsum("gce,fgc->fge", basis_blocks, grouped, precision=lax.Precision.HIGHEST)
    return turned.reshape(row_count, channels)


def local(
    ensemble,
    jacobian,
    innovation,
    error_vectors,
    error_values,
    ensemble_vectors,
    column_pick,
    footprint_slot,
    footprint_count,
):
    window = column_pick.shape[1]
    capacity = column_pick.shape[2]
    reach_tiles = window // 2
    level_part = ensemble.shape[1]
    members = ensemble.shape[2]
    chosen = jnp.take(ensemble, column_pick[0].reshape(-1), axis=0).reshape(
        window, capacity, level_part, members
    )
    blocks = []
    for slot_index in range(window):
        shift_by = slot_index - reach_tiles
        if shift_by == 0:
            blocks.append(chosen[slot_index])
        else:
            blocks.append(from_behind(chosen[slot_index], "tile", shift_by))
    arrived = jnp.stack(blocks, 0)
    slot_rows = arrived.reshape(window * capacity, level_part, members)
    columns = jnp.take(slot_rows, footprint_slot, axis=0)
    foot_rows = columns.shape[0]
    live_rows = (jnp.arange(foot_rows, dtype=jnp.int32) < footprint_count[0]).astype(jnp.float32)
    share_rows = foot_rows // lax.axis_size("chan")
    columns, sensitivity, misfit_rows = (
        lax.all_to_all(columns, "chan", split_axis=0, concat_axis=1, tiled=True),
        lax.all_to_all(jacobian, "chan", split_axis=0, concat_axis=1, tiled=True),
        lax.all_to_all(
            innovation.astype(jnp.bfloat16), "chan", split_axis=0, concat_axis=1, tiled=True
        ).astype(innovation.dtype),
    )
    response = jnp.einsum("fcl,flk->fck", sensitivity, columns, preferred_element_type=jnp.float32)
    row_weights = lax.dynamic_slice_in_dim(
        live_rows, lax.axis_index("chan") * share_rows, share_rows, 0
    )
    scales = 1.0 / jnp.sqrt(error_values)
    whitened = (
        turn_blocks(response, error_vectors) * scales[None, :, None] * row_weights[:, None, None]
    )
    misfit = turn_rows(misfit_rows, error_vectors) * scales[None, :]
    pull_sum = jnp.einsum("fck,fc->k", whitened, misfit, precision=lax.Precision.HIGHEST)
    rounded = whitened.astype(jnp.bfloat16).reshape(-1, members)
    gram_sum = lax.dot_general(
        rounded, rounded, (((0,), (0,)), ((), ())), preferred_element_type=jnp.float32
    )
    gram_sum, pull_sum = sum_all(gram_sum, pull_sum)
    system = gram_sum + (members - 1) * jnp.eye(members, dtype=jnp.float32)
    factor = jnp.linalg.cholesky(system)
    halfway = lax.linalg.triangular_solve(factor, pull_sum[:, None], left_side=True, lower=True)
    mean_weights = lax.linalg.triangular_solve(
        factor, halfway, left_side=True, lower=True, transpose_a=True
    )[:, 0]
    spread = jnp.sqrt(members - 1.0) * lax.linalg.triangular_solve(
        factor, ensemble_vectors, left_side=True, lower=True, transpose_a=True
    )
    transform = (spread + mean_weights[:, None]).astype(jnp.bfloat16)
    flat_rows = ensemble.reshape(-1, members)
    updated = apply_transform(flat_rows, transform)
    return updated.reshape(ensemble.shape)


def solution(mesh):
    return jax.shard_map(
        local,
        mesh=mesh,
        in_specs=(
            P("tile", "chan", None),
            P("tile", "chan", None),
            P("tile", "chan"),
            P(),
            P(),
            P(),
            P("tile", None, None),
            P("tile"),
            P("tile"),
        ),
        out_specs=P("tile", "chan", None),
        check_vma=False,
    )
```

```python
import functools
import jax
import jax.numpy as jnp
from jax import lax
from jax.experimental import pallas as pl
from jax.experimental.pallas import tpu as pltpu
from jax.sharding import PartitionSpec as P

MESH = pl.DeviceIdType.MESH


def greet(axes):
    barrier = pltpu.get_barrier_semaphore()
    total = 0
    for axis in axes:
        count = lax.axis_size(axis)
        here = lax.axis_index(axis)
        for step in range(1, count):
            pl.semaphore_signal(
                barrier, inc=1, device_id={axis: lax.rem(here + step, count)}, device_id_type=MESH
            )
        total += count - 1
    pl.semaphore_wait(barrier, total)


def sum_kernel(piece, x_ref, out_ref, landed, crossed, mine, summed, spread, sems_a, sems_b, sems_c):
    tiles = lax.axis_size("tile")
    chans = lax.axis_size("chan")
    tile = lax.axis_index("tile")
    chan = lax.axis_index("chan")
    greet(("tile", "chan"))

    def rows_of(index):
        return pl.ds(pl.multiple_of(index * piece, 8), piece)

    copies = []
    for step in range(1, tiles):
        peer = lax.rem(tile + step, tiles)
        copies.append(
            pltpu.make_async_remote_copy(
                src_ref=x_ref.at[rows_of(peer)],
                dst_ref=landed.at[step],
                send_sem=sems_a.at[0, step],
                recv_sem=sems_a.at[1, step],
                device_id={"tile": peer},
                device_id_type=MESH,
            )
        )
    for copy in copies:
        copy.start()
    total = x_ref[rows_of(tile), :]
    for step, copy in enumerate(copies, 1):
        copy.wait_recv()
        total = total + landed[step]
    mine[...] = total
    crossings = []
    for step in range(1, chans):
        crossings.append(
            pltpu.make_async_remote_copy(
                src_ref=mine,
                dst_ref=crossed.at[step],
                send_sem=sems_b.at[0, step],
                recv_sem=sems_b.at[1, step],
                device_id={"chan": lax.rem(chan + step, chans)},
                device_id_type=MESH,
            )
        )
    for copy in crossings:
        copy.start()
    for step, copy in enumerate(crossings, 1):
        copy.wait_recv()
        total = total + crossed[step]
    summed[...] = total
    shares = []
    for step in range(1, tiles):
        shares.append(
            pltpu.make_async_remote_copy(
                src_ref=summed,
                dst_ref=spread.at[step],
                send_sem=sems_c.at[0, step],
                recv_sem=sems_c.at[1, step],
                device_id={"tile": lax.rem(tile + step, tiles)},
                device_id_type=MESH,
            )
        )
    for copy in shares:
        copy.start()
    out_ref[rows_of(tile), :] = total
    for step, copy in enumerate(shares, 1):
        copy.wait_recv()
        out_ref[rows_of(lax.rem(tile - step + tiles, tiles)), :] = spread[step]
    for copy in copies + crossings + shares:
        copy.wait_send()


def sum_all(gram, pull):
    tiles = lax.axis_size("tile")
    chans = lax.axis_size("chan")
    members = gram.shape[0]
    half = members // 2
    used = 3 * half + 8
    piece = -(-used // (8 * tiles)) * 8
    flat = jnp.concatenate(
        [
            gram[:half, :half],
            gram[:half, half:],
            gram[half:, half:],
            pull.reshape(2, half),
            jnp.zeros((piece * tiles - 3 * half - 2, half), jnp.float32),
        ],
        0,
    )
    out = pl.pallas_call(
        functools.partial(sum_kernel, piece),
        out_shape=jax.ShapeDtypeStruct(flat.shape, jnp.float32),
        in_specs=[pl.BlockSpec(memory_space=pltpu.VMEM)],
        out_specs=pl.BlockSpec(memory_space=pltpu.VMEM),
        scratch_shapes=[
            pltpu.VMEM((tiles, piece, half), jnp.float32),
            pltpu.VMEM((chans, piece, half), jnp.float32),
            pltpu.VMEM((piece, half), jnp.float32),
            pltpu.VMEM((piece, half), jnp.float32),
            pltpu.VMEM((tiles, piece, half), jnp.float32),
            pltpu.SemaphoreType.DMA((2, tiles)),
            pltpu.SemaphoreType.DMA((2, chans)),
            pltpu.SemaphoreType.DMA((2, tiles)),
        ],
        compiler_params=pltpu.CompilerParams(collective_id=0, has_side_effects=True),
        name="sum_all",
    )(flat)
    top = out[:half]
    across = out[half : 2 * half]
    low = out[2 * half : 3 * half]
    gram = jnp.concatenate(
        [jnp.concatenate([top, across], 1), jnp.concatenate([across.T, low], 1)], 0
    )
    return gram, out[3 * half : 3 * half + 2].reshape(members)


def apply_kernel(x_ref, w_ref, o_ref):
    o_ref[...] = jnp.dot(x_ref[...], w_ref[...], preferred_element_type=jnp.float32).astype(o_ref.dtype)


def apply_transform(rows, transform):
    count, members = rows.shape
    block = min(count, 2048)
    while count % block:
        block //= 2
    return pl.pallas_call(
        apply_kernel,
        grid=(count // block,),
        out_shape=jax.ShapeDtypeStruct(rows.shape, rows.dtype),
        in_specs=[
            pl.BlockSpec((block, members), lambda i: (i, 0)),
            pl.BlockSpec((members, members), lambda i: (0, 0)),
        ],
        out_specs=pl.BlockSpec((block, members), lambda i: (i, 0)),
        name="apply_transform",
    )(rows, transform)


def exchange_kernel(
    window, cap, chunks, share,
    pick_ref, order_ref, slot_ref, live_ref, ens_ref, jac_ref, misfit_ref, high_ref, low_ref,
    gram_ref, pull_ref,
    ens_v, jac_s, jac_land, mis_land, mis_all, chosen, arr, col_s, col_land, white,
    ens_sem, sems_t, sems_j, sems_m, sems_c,
):
    chans = lax.axis_size("chan")
    tiles = lax.axis_size("tile")
    tile = lax.axis_index("tile")
    chan = lax.axis_index("chan")
    reach = window // 2
    level_part, members = ens_ref.shape[1], ens_ref.shape[2]
    part, levels = jac_ref.shape[1], jac_ref.shape[2]
    rows = chunks * share
    load = pltpu.make_async_copy(ens_ref, ens_v, ens_sem)
    load.start()

    def chan_peer(step):
        return lax.rem(chan + step, chans)

    def tile_peer(slot):
        return lax.rem(tile + slot - reach + tiles, tiles)

    barrier = pltpu.get_barrier_semaphore()
    for step in range(1, chans):
        pl.semaphore_signal(barrier, inc=1, device_id={"chan": chan_peer(step)}, device_id_type=MESH)
    for slot in range(window):
        if slot != reach:
            pl.semaphore_signal(barrier, inc=1, device_id={"tile": tile_peer(slot)}, device_id_type=MESH)

    jac_copies, mis_copies = [], []
    for step in range(1, chans):
        peer = chan_peer(step)

        def take_jac(i, carry, peer=peer):
            jac_s[peer, i] = jac_ref[order_ref[peer * rows + i]]
            return carry

        lax.fori_loop(0, rows, take_jac, 0)
        jac_copies.append(pltpu.make_async_remote_copy(
            src_ref=jac_s.at[peer], dst_ref=jac_land.at[chan],
            send_sem=sems_j.at[0, step], recv_sem=sems_j.at[1, step],
            device_id={"chan": peer}, device_id_type=MESH))
        mis_copies.append(pltpu.make_async_remote_copy(
            src_ref=misfit_ref.at[peer], dst_ref=mis_land.at[chan],
            send_sem=sems_m.at[0, step], recv_sem=sems_m.at[1, step],
            device_id={"chan": peer}, device_id_type=MESH))

    def own_jac(i, carry):
        jac_land[chan, i] = jac_ref[order_ref[chan * rows + i]]
        return carry

    lax.fori_loop(0, rows, own_jac, 0)
    mis_land[chan] = misfit_ref[chan]
    pl.semaphore_wait(barrier, chans - 1 + window - 1)
    for copy in mis_copies + jac_copies:
        copy.start()

    load.wait()
    offsets = sorted((s for s in range(window) if s != reach), key=lambda s: abs(s - reach))
    tile_copies = {}
    waiting = None
    for slot in offsets:
        def take_col(i, carry, slot=slot):
            chosen[slot, i] = ens_v[pick_ref[slot * cap + i]]
            return carry

        lax.fori_loop(0, cap, take_col, 0)
        if waiting is not None:
            waiting.start()
        waiting = tile_copies[slot] = pltpu.make_async_remote_copy(
            src_ref=chosen.at[slot], dst_ref=arr[slot],
            send_sem=sems_t.at[0, slot], recv_sem=sems_t.at[1, slot],
            device_id={"tile": tile_peer(slot)}, device_id_type=MESH)

    def own_col(i, carry):
        arr[reach][i] = ens_v[pick_ref[reach * cap + i]]
        return carry

    lax.fori_loop(0, cap, own_col, 0)
    waiting.start()

    landed = {reach}
    col_copies = {}

    def send_chunk(q):
        for slot in (q, q + 1):
            if slot not in landed:
                tile_copies[slot].wait_recv()
                landed.add(slot)

        def pick(peer, i):
            index = slot_ref[peer * rows + q * share + i] - q * cap
            near = arr[q][jnp.clip(index, 0, cap - 1)]
            far = arr[q + 1][jnp.clip(index - cap, 0, cap - 1)]
            return lax.select(index < cap, near, far)

        waiting = None
        for step in range(1, chans):
            peer = chan_peer(step)

            def take(i, carry, peer=peer):
                col_s[peer, q, i] = pick(peer, i)
                return carry

            lax.fori_loop(0, share, take, 0)
            if waiting is not None:
                waiting.start()
            waiting = col_copies[q, step] = pltpu.make_async_remote_copy(
                src_ref=col_s.at[peer, q], dst_ref=col_land.at[chan, q],
                send_sem=sems_c.at[0, q, step], recv_sem=sems_c.at[1, q, step],
                device_id={"chan": peer}, device_id_type=MESH)

        def own(i, carry):
            col_land[chan, q, i] = pick(chan, i)
            return carry

        lax.fori_loop(0, share, own, 0)
        waiting.start()

    sequence = sorted(range(chunks), key=lambda q: max(abs(q - reach), abs(q + 1 - reach)))
    half = len(sequence) // 2
    for q in sequence[:half]:
        send_chunk(q)

    for copy in mis_copies + jac_copies:
        copy.wait_recv()
    total = mis_land[0]
    for z in range(1, chans):
        total = total + mis_land[z]
    mis_all[...] = total

    def whiten(i, carry):
        block = jac_land[:, i].reshape(chans * part, levels)
        turned = jnp.dot(high_ref[...], block, preferred_element_type=jnp.float32)
        turned = turned + jnp.dot(low_ref[...], block, preferred_element_type=jnp.float32)
        turned = turned * live_ref[chan * rows + i]
        first = turned.astype(jnp.bfloat16)
        white[i, :, :levels] = first
        white[i, :, levels:] = (turned - first.astype(jnp.float32)).astype(jnp.bfloat16)
        return carry

    lax.fori_loop(0, rows, whiten, 0)
    for q in sequence[half:]:
        send_chunk(q)

    gram_ref[...] = jnp.zeros_like(gram_ref)
    pull_ref[...] = jnp.zeros_like(pull_ref)
    channels = chans * part
    pair = 2 if share % 2 == 0 else 1

    for q in sequence:
        for step in range(1, chans):
            col_copies[q, step].wait_recv()

        def add(i, carry, q=q):
            rounded, weights = [], []
            for k in range(pair):
                s = i * pair + k
                block = col_land[:, q, s].reshape(levels, members)
                both = jnp.concatenate([block, block], 0)
                rounded.append(
                    jnp.dot(white[q * share + s], both, preferred_element_type=jnp.float32).astype(jnp.bfloat16)
                )
                weights.append(mis_all[pl.ds(q * share + s, 1), :])
            rounded = jnp.concatenate(rounded, 0)
            weights = jnp.broadcast_to(jnp.concatenate(weights, 1), (8, pair * channels))
            first = weights.astype(jnp.bfloat16).astype(jnp.float32)
            line = lax.broadcasted_iota(jnp.int32, weights.shape, 0)
            left = jnp.where(line == 0, first, jnp.where(line == 1, weights - first, 0.0))
            pull_ref[...] += jnp.dot(left.astype(jnp.bfloat16), rounded, preferred_element_type=jnp.float32)
            gram_ref[...] += lax.dot_general(
                rounded, rounded, (((0,), (0,)), ((), ())), preferred_element_type=jnp.float32
            )
            return carry

        lax.fori_loop(0, share // pair, add, 0)
    for copy in mis_copies + jac_copies + list(tile_copies.values()) + list(col_copies.values()):
        copy.wait_send()


def fits(ensemble, jacobian, column_pick, footprint_slot):
    chans = lax.axis_size("chan")
    window, cap = column_pick.shape[1:]
    return (
        footprint_slot.shape[0] == (window - 1) * cap
        and cap % chans == 0
        and window <= lax.axis_size("tile")
        and ensemble.shape[1] % 16 == 0
        and jacobian.shape[1] % 16 == 0
        and ensemble.shape[1] * chans == jacobian.shape[2]
        and jacobian.shape[1] * chans == jacobian.shape[2]
        and jacobian.shape[2] % 128 == 0
    )


def exchange(ensemble, jacobian, innovation, error_vectors, error_values, column_pick, footprint_slot, footprint_count):
    chans = lax.axis_size("chan")
    chan = lax.axis_index("chan")
    window, cap = column_pick.shape[1:]
    foot_rows = footprint_slot.shape[0]
    chunks = window - 1
    share = cap // chans
    rows = chunks * share
    part, levels = jacobian.shape[1:]
    level_part, members = ensemble.shape[1:]
    channels = part * chans
    group = error_vectors.shape[1]
    rank = jnp.sum(footprint_slot[None, :] < footprint_slot[:, None], axis=1, dtype=jnp.int32)
    place = jnp.arange(foot_rows, dtype=jnp.int32)
    spot = place % rows
    wanted = (spot // share) * cap + (place // rows) * share + spot % share
    match = rank[None, :] == wanted[:, None]
    order = jnp.sum(jnp.where(match, place[None, :], 0), axis=1)
    slots = jnp.sum(jnp.where(match, footprint_slot[None, :], 0), axis=1)
    live = (order < footprint_count[0]).astype(jnp.float32)
    spread = jnp.tile(error_vectors, (1, channels // group))
    group_of = jnp.arange(channels) // group
    basis = jnp.where(group_of[:, None] == group_of[None, :], spread, 0.0) / jnp.sqrt(error_values)[None, :]
    turned = basis.T
    high = turned.astype(jnp.bfloat16)
    low = (turned - high.astype(jnp.float32)).astype(jnp.bfloat16)
    ours = lax.dynamic_slice_in_dim(basis, chan * part, part, 0)
    misfit = jnp.dot(innovation, ours, precision=lax.Precision.HIGHEST)
    misfit = jnp.dot(match.astype(jnp.float32), misfit, precision=lax.Precision.HIGHEST)
    misfit = misfit.reshape(chans, rows, channels)
    vmem = pl.BlockSpec(memory_space=pltpu.VMEM)
    smem = pl.BlockSpec(memory_space=pltpu.SMEM)
    half = jnp.bfloat16
    gram, pull = pl.pallas_call(
        functools.partial(exchange_kernel, window, cap, chunks, share),
        out_shape=(
            jax.ShapeDtypeStruct((members, members), jnp.float32),
            jax.ShapeDtypeStruct((8, members), jnp.float32),
        ),
        in_specs=[smem] * 4 + [pl.BlockSpec(memory_space=pl.ANY)] + [vmem] * 4,
        out_specs=(vmem, vmem),
        scratch_shapes=[
            pltpu.VMEM(ensemble.shape, half),
            pltpu.VMEM((chans, rows, part, levels), half),
            pltpu.VMEM((chans, rows, part, levels), half),
            pltpu.VMEM((chans, rows, channels), jnp.float32),
            pltpu.VMEM((rows, channels), jnp.float32),
            pltpu.VMEM((window, cap, level_part, members), half),
            [pltpu.VMEM((cap, level_part, members), half) for _ in range(window)],
            pltpu.VMEM((chans, chunks, share, level_part, members), half),
            pltpu.VMEM((chans, chunks, share, level_part, members), half),
            pltpu.VMEM((rows, channels, 2 * levels), half),
            pltpu.SemaphoreType.DMA,
            pltpu.SemaphoreType.DMA((2, window)),
            pltpu.SemaphoreType.DMA((2, chans)),
            pltpu.SemaphoreType.DMA((2, chans)),
            pltpu.SemaphoreType.DMA((2, chunks, chans)),
        ],
        compiler_params=pltpu.CompilerParams(
            collective_id=1, has_side_effects=True, vmem_limit_bytes=48 * 1024 * 1024
        ),
        name="exchange",
    )(column_pick.reshape(-1), order, slots, live, ensemble, jacobian, misfit, high, low)
    return gram, pull[0] + pull[1]


def from_behind(value, axis, steps):
    count = lax.axis_size(axis)
    pairs = [(source, (source + steps) % count) for source in range(count)]
    return lax.ppermute(value, axis, pairs)


def turn_blocks(values, vectors):
    row_count, channels, members = values.shape
    group_width = vectors.shape[1]
    grouped = values.reshape(row_count, channels // group_width, group_width, members)
    basis_blocks = vectors.reshape(channels // group_width, group_width, group_width)
    turned = jnp.einsum("gce,fgck->fgek", basis_blocks, grouped, precision=lax.Precision.HIGHEST)
    return turned.reshape(row_count, channels, members)


def turn_rows(values, vectors):
    row_count, channels = values.shape
    group_width = vectors.shape[1]
    grouped = values.reshape(row_count, channels // group_width, group_width)
    basis_blocks = vectors.reshape(channels // group_width, group_width, group_width)
    turned = jnp.einsum("gce,fgc->fge", basis_blocks, grouped, precision=lax.Precision.HIGHEST)
    return turned.reshape(row_count, channels)


def exchange_plain(
    ensemble, jacobian, innovation, error_vectors, error_values, column_pick, footprint_slot, footprint_count
):
    window = column_pick.shape[1]
    capacity = column_pick.shape[2]
    reach_tiles = window // 2
    level_part = ensemble.shape[1]
    members = ensemble.shape[2]
    chosen = jnp.take(ensemble, column_pick[0].reshape(-1), axis=0).reshape(
        window, capacity, level_part, members
    )
    blocks = []
    for slot_index in range(window):
        shift_by = slot_index - reach_tiles
        if shift_by == 0:
            blocks.append(chosen[slot_index])
        else:
            blocks.append(from_behind(chosen[slot_index], "tile", shift_by))
    arrived = jnp.stack(blocks, 0)
    slot_rows = arrived.reshape(window * capacity, level_part, members)
    columns = jnp.take(slot_rows, footprint_slot, axis=0)
    foot_rows = columns.shape[0]
    live_rows = (jnp.arange(foot_rows, dtype=jnp.int32) < footprint_count[0]).astype(jnp.float32)
    share_rows = foot_rows // lax.axis_size("chan")
    columns, sensitivity, misfit_rows = (
        lax.all_to_all(columns, "chan", split_axis=0, concat_axis=1, tiled=True),
        lax.all_to_all(jacobian, "chan", split_axis=0, concat_axis=1, tiled=True),
        lax.all_to_all(
            innovation.astype(jnp.bfloat16), "chan", split_axis=0, concat_axis=1, tiled=True
        ).astype(innovation.dtype),
    )
    response = jnp.einsum("fcl,flk->fck", sensitivity, columns, preferred_element_type=jnp.float32)
    row_weights = lax.dynamic_slice_in_dim(
        live_rows, lax.axis_index("chan") * share_rows, share_rows, 0
    )
    scales = 1.0 / jnp.sqrt(error_values)
    whitened = (
        turn_blocks(response, error_vectors) * scales[None, :, None] * row_weights[:, None, None]
    )
    misfit = turn_rows(misfit_rows, error_vectors) * scales[None, :]
    pull_sum = jnp.einsum("fck,fc->k", whitened, misfit, precision=lax.Precision.HIGHEST)
    rounded = whitened.astype(jnp.bfloat16).reshape(-1, members)
    gram_sum = lax.dot_general(
        rounded, rounded, (((0,), (0,)), ((), ())), preferred_element_type=jnp.float32
    )
    return gram_sum, pull_sum


def local(
    ensemble,
    jacobian,
    innovation,
    error_vectors,
    error_values,
    ensemble_vectors,
    column_pick,
    footprint_slot,
    footprint_count,
):
    members = ensemble.shape[2]
    route = exchange if fits(ensemble, jacobian, column_pick, footprint_slot) else exchange_plain
    gram_sum, pull_sum = route(
        ensemble, jacobian, innovation, error_vectors, error_values, column_pick, footprint_slot, footprint_count
    )
    gram_sum, pull_sum = sum_all(gram_sum, pull_sum)
    system = gram_sum + (members - 1) * jnp.eye(members, dtype=jnp.float32)
    factor = jnp.linalg.cholesky(system)
    halfway = lax.linalg.triangular_solve(factor, pull_sum[:, None], left_side=True, lower=True)
    mean_weights = lax.linalg.triangular_solve(
        factor, halfway, left_side=True, lower=True, transpose_a=True
    )[:, 0]
    spread = jnp.sqrt(members - 1.0) * lax.linalg.triangular_solve(
        factor, ensemble_vectors, left_side=True, lower=True, transpose_a=True
    )
    transform = (spread + mean_weights[:, None]).astype(jnp.bfloat16)
    flat_rows = ensemble.reshape(-1, members)
    updated = apply_transform(flat_rows, transform)
    return updated.reshape(ensemble.shape)


def solution(mesh):
    return jax.shard_map(
        local,
        mesh=mesh,
        in_specs=(
            P("tile", "chan", None),
            P("tile", "chan", None),
            P("tile", "chan"),
            P(),
            P(),
            P(),
            P("tile", None, None),
            P("tile"),
            P("tile"),
        ),
        out_specs=P("tile", "chan", None),
        check_vma=False,
    )
```

```python
import functools
import jax
import jax.numpy as jnp
from jax import lax
from jax.experimental import pallas as pl
from jax.experimental.pallas import tpu as pltpu
from jax.sharding import PartitionSpec as P

MESH = pl.DeviceIdType.MESH


def greet(axes):
    barrier = pltpu.get_barrier_semaphore()
    total = 0
    for axis in axes:
        count = lax.axis_size(axis)
        here = lax.axis_index(axis)
        for step in range(1, count):
            pl.semaphore_signal(
                barrier, inc=1, device_id={axis: lax.rem(here + step, count)}, device_id_type=MESH
            )
        total += count - 1
    pl.semaphore_wait(barrier, total)


def sum_kernel(piece, x_ref, out_ref, landed, crossed, mine, summed, spread, sems_a, sems_b, sems_c):
    tiles = lax.axis_size("tile")
    chans = lax.axis_size("chan")
    tile = lax.axis_index("tile")
    chan = lax.axis_index("chan")
    greet(("tile", "chan"))

    def rows_of(index):
        return pl.ds(pl.multiple_of(index * piece, 8), piece)

    copies = []
    for step in range(1, tiles):
        peer = lax.rem(tile + step, tiles)
        copies.append(
            pltpu.make_async_remote_copy(
                src_ref=x_ref.at[rows_of(peer)],
                dst_ref=landed.at[step],
                send_sem=sems_a.at[0, step],
                recv_sem=sems_a.at[1, step],
                device_id={"tile": peer},
                device_id_type=MESH,
            )
        )
    for copy in copies:
        copy.start()
    total = x_ref[rows_of(tile), :]
    for step, copy in enumerate(copies, 1):
        copy.wait_recv()
        total = total + landed[step]
    mine[...] = total
    crossings = []
    for step in range(1, chans):
        crossings.append(
            pltpu.make_async_remote_copy(
                src_ref=mine,
                dst_ref=crossed.at[step],
                send_sem=sems_b.at[0, step],
                recv_sem=sems_b.at[1, step],
                device_id={"chan": lax.rem(chan + step, chans)},
                device_id_type=MESH,
            )
        )
    for copy in crossings:
        copy.start()
    for step, copy in enumerate(crossings, 1):
        copy.wait_recv()
        total = total + crossed[step]
    summed[...] = total
    shares = []
    for step in range(1, tiles):
        shares.append(
            pltpu.make_async_remote_copy(
                src_ref=summed,
                dst_ref=spread.at[step],
                send_sem=sems_c.at[0, step],
                recv_sem=sems_c.at[1, step],
                device_id={"tile": lax.rem(tile + step, tiles)},
                device_id_type=MESH,
            )
        )
    for copy in shares:
        copy.start()
    out_ref[rows_of(tile), :] = total
    for step, copy in enumerate(shares, 1):
        copy.wait_recv()
        out_ref[rows_of(lax.rem(tile - step + tiles, tiles)), :] = spread[step]
    for copy in copies + crossings + shares:
        copy.wait_send()


def sum_all(gram, pull):
    tiles = lax.axis_size("tile")
    chans = lax.axis_size("chan")
    members = gram.shape[0]
    half = members // 2
    used = 3 * half + 8
    piece = -(-used // (8 * tiles)) * 8
    flat = jnp.concatenate(
        [
            gram[:half, :half],
            gram[:half, half:],
            gram[half:, half:],
            pull.reshape(2, half),
            jnp.zeros((piece * tiles - 3 * half - 2, half), jnp.float32),
        ],
        0,
    )
    return pl.pallas_call(
        functools.partial(sum_kernel, piece),
        out_shape=jax.ShapeDtypeStruct(flat.shape, jnp.float32),
        in_specs=[pl.BlockSpec(memory_space=pltpu.VMEM)],
        out_specs=pl.BlockSpec(memory_space=pltpu.VMEM),
        scratch_shapes=[
            pltpu.VMEM((tiles, piece, half), jnp.float32),
            pltpu.VMEM((chans, piece, half), jnp.float32),
            pltpu.VMEM((piece, half), jnp.float32),
            pltpu.VMEM((piece, half), jnp.float32),
            pltpu.VMEM((tiles, piece, half), jnp.float32),
            pltpu.SemaphoreType.DMA((2, tiles)),
            pltpu.SemaphoreType.DMA((2, chans)),
            pltpu.SemaphoreType.DMA((2, tiles)),
        ],
        compiler_params=pltpu.CompilerParams(collective_id=0, has_side_effects=True),
        name="sum_all",
    )(flat)


def invert_factor(d_ref, y_ref):
    size = d_ref.shape[0]
    step = 8
    shape = d_ref.shape
    y_ref[...] = (
        lax.broadcasted_iota(jnp.int32, shape, 0) == lax.broadcasted_iota(jnp.int32, shape, 1)
    ).astype(jnp.float32)
    for start in range(0, size, step):
        below = d_ref[start:, :]
        right = y_ref[start:, :]
        line = lax.broadcasted_iota(jnp.int32, below.shape, 0)
        columns = [
            jnp.broadcast_to(below[:, start + j : start + j + 1], below.shape) for j in range(step)
        ]
        rows = [below[j : j + 1, :] for j in range(step)]
        others = [right[j : j + 1, :] for j in range(step)]
        for j in range(step):
            pivot = columns[j][j : j + 1, :]
            inverse = 1.0 / pivot
            under = jnp.where(line > j, columns[j], 0.0)
            row = rows[j] * inverse
            other = others[j] * inverse
            for k in range(j + 1, step):
                entry = columns[j][k : k + 1, :]
                columns[k] = columns[k] - under * (columns[k][j : j + 1, :] * inverse)
                rows[k] = rows[k] - entry * row
                others[k] = others[k] - entry * other
            below = below - under * row
            right = right - under * other
            y_ref[start + j : start + j + 1, :] = others[j] * (1.0 / jnp.sqrt(pivot))
        if start + step < size:
            d_ref[start + step :, :] = below[step:, :]
            y_ref[start + step :, :] = right[step:, :]


def finish_kernel(pieces, sum_ref, vec_ref, ens_ref, out_ref, d_ref, first, second, ens_v, out_v, load_sem, sems):
    half = d_ref.shape[0]
    members = 2 * half
    load = pltpu.make_async_copy(ens_ref, ens_v, load_sem)
    load.start()
    dims = lambda a, b: (((a,), (b,)), ((), ()))

    def dot(x, y, a=1, b=0):
        return lax.dot_general(
            x, y, dims(a, b), precision=lax.Precision.HIGHEST, preferred_element_type=jnp.float32
        )

    eye = (
        lax.broadcasted_iota(jnp.int32, (half, half), 0) == lax.broadcasted_iota(jnp.int32, (half, half), 1)
    ).astype(jnp.float32) * (members - 1)
    d_ref[...] = sum_ref[:half, :] + eye
    invert_factor(d_ref, first)
    across = dot(first[...], sum_ref[half : 2 * half, :])
    d_ref[...] = sum_ref[2 * half : 3 * half, :] + eye - dot(across, across, 0, 0)
    invert_factor(d_ref, second)
    low = -dot(second[...], dot(across, first[...], 0, 0))
    pull = sum_ref[3 * half : 3 * half + 8, :]
    top_half = jnp.sum(first[...] * pull[0:1, :], axis=1, keepdims=True)
    low_half = jnp.sum(low * pull[0:1, :] + second[...] * pull[1:2, :], axis=1, keepdims=True)
    scale = float(members - 1) ** 0.5
    top_right = scale * vec_ref[:half, :] + top_half
    low_right = scale * vec_ref[half:, :] + low_half
    transform = jnp.concatenate(
        [dot(first[...], top_right, 0, 0) + dot(low, low_right, 0, 0), dot(second[...], low_right, 0, 0)], 0
    ).astype(jnp.bfloat16)
    load.wait()
    size = ens_ref.shape[0] // pieces
    writes = []
    for i in range(pieces):
        span = pl.ds(i * size, size)
        out_v[span, :] = jnp.dot(
            ens_v[span, :], transform, preferred_element_type=jnp.float32
        ).astype(jnp.bfloat16)
        writes.append(pltpu.make_async_copy(out_v.at[span], out_ref.at[span], sems.at[i]))
        writes[-1].start()
    for write in writes:
        write.wait()


def finish(sums, ensemble_vectors, rows):
    members = ensemble_vectors.shape[0]
    half = members // 2
    pieces = 8
    vmem = pl.BlockSpec(memory_space=pltpu.VMEM)
    return pl.pallas_call(
        functools.partial(finish_kernel, pieces),
        out_shape=jax.ShapeDtypeStruct(rows.shape, rows.dtype),
        in_specs=[vmem, vmem, pl.BlockSpec(memory_space=pl.ANY)],
        out_specs=pl.BlockSpec(memory_space=pl.ANY),
        scratch_shapes=[
            pltpu.VMEM((half, half), jnp.float32),
            pltpu.VMEM((half, half), jnp.float32),
            pltpu.VMEM((half, half), jnp.float32),
            pltpu.VMEM(rows.shape, rows.dtype),
            pltpu.VMEM(rows.shape, rows.dtype),
            pltpu.SemaphoreType.DMA,
            pltpu.SemaphoreType.DMA((pieces,)),
        ],
        compiler_params=pltpu.CompilerParams(vmem_limit_bytes=40 * 1024 * 1024),
        name="finish",
    )(sums, ensemble_vectors, rows)


def exchange_kernel(
    window, cap, chunks, share,
    pick_ref, order_ref, slot_ref, live_ref, ens_ref, jac_ref, misfit_ref, high_ref, low_ref,
    gram_ref, pull_ref,
    ens_v, jac_s, jac_land, mis_land, mis_all, chosen, arr, col_s, col_land, white,
    ens_sem, sems_t, sems_j, sems_m, sems_c,
):
    chans = lax.axis_size("chan")
    tiles = lax.axis_size("tile")
    tile = lax.axis_index("tile")
    chan = lax.axis_index("chan")
    reach = window // 2
    level_part, members = ens_ref.shape[1], ens_ref.shape[2]
    part, levels = jac_ref.shape[1], jac_ref.shape[2]
    rows = chunks * share
    load = pltpu.make_async_copy(ens_ref, ens_v, ens_sem)
    load.start()

    def chan_peer(step):
        return lax.rem(chan + step, chans)

    def tile_peer(slot):
        return lax.rem(tile + slot - reach + tiles, tiles)

    barrier = pltpu.get_barrier_semaphore()
    for step in range(1, chans):
        pl.semaphore_signal(barrier, inc=1, device_id={"chan": chan_peer(step)}, device_id_type=MESH)
    for slot in range(window):
        if slot != reach:
            pl.semaphore_signal(barrier, inc=1, device_id={"tile": tile_peer(slot)}, device_id_type=MESH)

    jac_copies, mis_copies = [], []
    for step in range(1, chans):
        peer = chan_peer(step)

        def take_jac(i, carry, peer=peer):
            jac_s[peer, i] = jac_ref[order_ref[peer * rows + i]]
            return carry

        lax.fori_loop(0, rows, take_jac, 0)
        jac_copies.append(pltpu.make_async_remote_copy(
            src_ref=jac_s.at[peer], dst_ref=jac_land.at[chan],
            send_sem=sems_j.at[0, step], recv_sem=sems_j.at[1, step],
            device_id={"chan": peer}, device_id_type=MESH))
        mis_copies.append(pltpu.make_async_remote_copy(
            src_ref=misfit_ref.at[peer], dst_ref=mis_land.at[chan],
            send_sem=sems_m.at[0, step], recv_sem=sems_m.at[1, step],
            device_id={"chan": peer}, device_id_type=MESH))

    def own_jac(i, carry):
        jac_land[chan, i] = jac_ref[order_ref[chan * rows + i]]
        return carry

    lax.fori_loop(0, rows, own_jac, 0)
    mis_land[chan] = misfit_ref[chan]
    pl.semaphore_wait(barrier, chans - 1 + window - 1)
    for copy in mis_copies + jac_copies:
        copy.start()

    load.wait()
    offsets = sorted((s for s in range(window) if s != reach), key=lambda s: abs(s - reach))
    tile_copies = {}
    waiting = None
    for slot in offsets:
        def take_col(i, carry, slot=slot):
            chosen[slot, i] = ens_v[pick_ref[slot * cap + i]]
            return carry

        lax.fori_loop(0, cap, take_col, 0)
        if waiting is not None:
            waiting.start()
        waiting = tile_copies[slot] = pltpu.make_async_remote_copy(
            src_ref=chosen.at[slot], dst_ref=arr[slot],
            send_sem=sems_t.at[0, slot], recv_sem=sems_t.at[1, slot],
            device_id={"tile": tile_peer(slot)}, device_id_type=MESH)

    def own_col(i, carry):
        arr[reach][i] = ens_v[pick_ref[reach * cap + i]]
        return carry

    lax.fori_loop(0, cap, own_col, 0)
    waiting.start()

    landed = {reach}
    col_copies = {}

    def send_chunk(q):
        for slot in (q, q + 1):
            if slot not in landed:
                tile_copies[slot].wait_recv()
                landed.add(slot)

        def pick(peer, i):
            index = slot_ref[peer * rows + q * share + i] - q * cap
            near = arr[q][jnp.clip(index, 0, cap - 1)]
            far = arr[q + 1][jnp.clip(index - cap, 0, cap - 1)]
            return lax.select(index < cap, near, far)

        waiting = None
        for step in range(1, chans):
            peer = chan_peer(step)

            def take(i, carry, peer=peer):
                col_s[peer, q, i] = pick(peer, i)
                return carry

            lax.fori_loop(0, share, take, 0)
            if waiting is not None:
                waiting.start()
            waiting = col_copies[q, step] = pltpu.make_async_remote_copy(
                src_ref=col_s.at[peer, q], dst_ref=col_land.at[chan, q],
                send_sem=sems_c.at[0, q, step], recv_sem=sems_c.at[1, q, step],
                device_id={"chan": peer}, device_id_type=MESH)

        def own(i, carry):
            col_land[chan, q, i] = pick(chan, i)
            return carry

        lax.fori_loop(0, share, own, 0)
        waiting.start()

    sequence = sorted(range(chunks), key=lambda q: max(abs(q - reach), abs(q + 1 - reach)))
    half = len(sequence) // 2
    for q in sequence[:half]:
        send_chunk(q)

    for copy in mis_copies + jac_copies:
        copy.wait_recv()
    total = mis_land[0]
    for z in range(1, chans):
        total = total + mis_land[z]
    mis_all[...] = total

    def whiten(i, carry):
        block = jac_land[:, i].reshape(chans * part, levels)
        turned = jnp.dot(high_ref[...], block, preferred_element_type=jnp.float32)
        turned = turned + jnp.dot(low_ref[...], block, preferred_element_type=jnp.float32)
        turned = turned * live_ref[chan * rows + i]
        first = turned.astype(jnp.bfloat16)
        white[i, :, :levels] = first
        white[i, :, levels:] = (turned - first.astype(jnp.float32)).astype(jnp.bfloat16)
        return carry

    lax.fori_loop(0, rows, whiten, 0)
    for q in sequence[half:]:
        send_chunk(q)

    gram_ref[...] = jnp.zeros_like(gram_ref)
    pull_ref[...] = jnp.zeros_like(pull_ref)
    channels = chans * part
    pair = 2 if share % 2 == 0 else 1

    for q in sequence:
        for step in range(1, chans):
            col_copies[q, step].wait_recv()

        def add(i, carry, q=q):
            rounded, weights = [], []
            for k in range(pair):
                s = i * pair + k
                block = col_land[:, q, s].reshape(levels, members)
                both = jnp.concatenate([block, block], 0)
                rounded.append(
                    jnp.dot(white[q * share + s], both, preferred_element_type=jnp.float32).astype(jnp.bfloat16)
                )
                weights.append(mis_all[pl.ds(q * share + s, 1), :])
            rounded = jnp.concatenate(rounded, 0)
            weights = jnp.broadcast_to(jnp.concatenate(weights, 1), (8, pair * channels))
            first = weights.astype(jnp.bfloat16).astype(jnp.float32)
            line = lax.broadcasted_iota(jnp.int32, weights.shape, 0)
            left = jnp.where(line == 0, first, jnp.where(line == 1, weights - first, 0.0))
            pull_ref[...] += jnp.dot(left.astype(jnp.bfloat16), rounded, preferred_element_type=jnp.float32)
            gram_ref[...] += lax.dot_general(
                rounded, rounded, (((0,), (0,)), ((), ())), preferred_element_type=jnp.float32
            )
            return carry

        lax.fori_loop(0, share // pair, add, 0)
    for copy in mis_copies + jac_copies + list(tile_copies.values()) + list(col_copies.values()):
        copy.wait_send()


def fits(ensemble, jacobian, column_pick, footprint_slot):
    chans = lax.axis_size("chan")
    window, cap = column_pick.shape[1:]
    return (
        footprint_slot.shape[0] == (window - 1) * cap
        and cap % chans == 0
        and window <= lax.axis_size("tile")
        and ensemble.shape[1] % 16 == 0
        and jacobian.shape[1] % 16 == 0
        and ensemble.shape[1] * chans == jacobian.shape[2]
        and jacobian.shape[1] * chans == jacobian.shape[2]
        and jacobian.shape[2] % 128 == 0
    )


def exchange(ensemble, jacobian, innovation, error_vectors, error_values, column_pick, footprint_slot, footprint_count):
    chans = lax.axis_size("chan")
    chan = lax.axis_index("chan")
    window, cap = column_pick.shape[1:]
    foot_rows = footprint_slot.shape[0]
    chunks = window - 1
    share = cap // chans
    rows = chunks * share
    part, levels = jacobian.shape[1:]
    level_part, members = ensemble.shape[1:]
    channels = part * chans
    group = error_vectors.shape[1]
    rank = jnp.sum(footprint_slot[None, :] < footprint_slot[:, None], axis=1, dtype=jnp.int32)
    place = jnp.arange(foot_rows, dtype=jnp.int32)
    spot = place % rows
    wanted = (spot // share) * cap + (place // rows) * share + spot % share
    match = rank[None, :] == wanted[:, None]
    order = jnp.sum(jnp.where(match, place[None, :], 0), axis=1)
    slots = jnp.sum(jnp.where(match, footprint_slot[None, :], 0), axis=1)
    live = (order < footprint_count[0]).astype(jnp.float32)
    spread = jnp.tile(error_vectors, (1, channels // group))
    group_of = jnp.arange(channels) // group
    basis = jnp.where(group_of[:, None] == group_of[None, :], spread, 0.0) / jnp.sqrt(error_values)[None, :]
    turned = basis.T
    high = turned.astype(jnp.bfloat16)
    low = (turned - high.astype(jnp.float32)).astype(jnp.bfloat16)
    ours = lax.dynamic_slice_in_dim(basis, chan * part, part, 0)
    misfit = jnp.dot(innovation, ours, precision=lax.Precision.HIGHEST)
    misfit = jnp.dot(match.astype(jnp.float32), misfit, precision=lax.Precision.HIGHEST)
    misfit = misfit.reshape(chans, rows, channels)
    vmem = pl.BlockSpec(memory_space=pltpu.VMEM)
    smem = pl.BlockSpec(memory_space=pltpu.SMEM)
    half = jnp.bfloat16
    gram, pull = pl.pallas_call(
        functools.partial(exchange_kernel, window, cap, chunks, share),
        out_shape=(
            jax.ShapeDtypeStruct((members, members), jnp.float32),
            jax.ShapeDtypeStruct((8, members), jnp.float32),
        ),
        in_specs=[smem] * 4 + [pl.BlockSpec(memory_space=pl.ANY)] + [vmem] * 4,
        out_specs=(vmem, vmem),
        scratch_shapes=[
            pltpu.VMEM(ensemble.shape, half),
            pltpu.VMEM((chans, rows, part, levels), half),
            pltpu.VMEM((chans, rows, part, levels), half),
            pltpu.VMEM((chans, rows, channels), jnp.float32),
            pltpu.VMEM((rows, channels), jnp.float32),
            pltpu.VMEM((window, cap, level_part, members), half),
            [pltpu.VMEM((cap, level_part, members), half) for _ in range(window)],
            pltpu.VMEM((chans, chunks, share, level_part, members), half),
            pltpu.VMEM((chans, chunks, share, level_part, members), half),
            pltpu.VMEM((rows, channels, 2 * levels), half),
            pltpu.SemaphoreType.DMA,
            pltpu.SemaphoreType.DMA((2, window)),
            pltpu.SemaphoreType.DMA((2, chans)),
            pltpu.SemaphoreType.DMA((2, chans)),
            pltpu.SemaphoreType.DMA((2, chunks, chans)),
        ],
        compiler_params=pltpu.CompilerParams(
            collective_id=1, has_side_effects=True, vmem_limit_bytes=48 * 1024 * 1024
        ),
        name="exchange",
    )(column_pick.reshape(-1), order, slots, live, ensemble, jacobian, misfit, high, low)
    return gram, pull[0] + pull[1]


def from_behind(value, axis, steps):
    count = lax.axis_size(axis)
    pairs = [(source, (source + steps) % count) for source in range(count)]
    return lax.ppermute(value, axis, pairs)


def turn_blocks(values, vectors):
    row_count, channels, members = values.shape
    group_width = vectors.shape[1]
    grouped = values.reshape(row_count, channels // group_width, group_width, members)
    basis_blocks = vectors.reshape(channels // group_width, group_width, group_width)
    turned = jnp.einsum("gce,fgck->fgek", basis_blocks, grouped, precision=lax.Precision.HIGHEST)
    return turned.reshape(row_count, channels, members)


def turn_rows(values, vectors):
    row_count, channels = values.shape
    group_width = vectors.shape[1]
    grouped = values.reshape(row_count, channels // group_width, group_width)
    basis_blocks = vectors.reshape(channels // group_width, group_width, group_width)
    turned = jnp.einsum("gce,fgc->fge", basis_blocks, grouped, precision=lax.Precision.HIGHEST)
    return turned.reshape(row_count, channels)


def exchange_plain(
    ensemble, jacobian, innovation, error_vectors, error_values, column_pick, footprint_slot, footprint_count
):
    window = column_pick.shape[1]
    capacity = column_pick.shape[2]
    reach_tiles = window // 2
    level_part = ensemble.shape[1]
    members = ensemble.shape[2]
    chosen = jnp.take(ensemble, column_pick[0].reshape(-1), axis=0).reshape(
        window, capacity, level_part, members
    )
    blocks = []
    for slot_index in range(window):
        shift_by = slot_index - reach_tiles
        if shift_by == 0:
            blocks.append(chosen[slot_index])
        else:
            blocks.append(from_behind(chosen[slot_index], "tile", shift_by))
    arrived = jnp.stack(blocks, 0)
    slot_rows = arrived.reshape(window * capacity, level_part, members)
    columns = jnp.take(slot_rows, footprint_slot, axis=0)
    foot_rows = columns.shape[0]
    live_rows = (jnp.arange(foot_rows, dtype=jnp.int32) < footprint_count[0]).astype(jnp.float32)
    share_rows = foot_rows // lax.axis_size("chan")
    columns, sensitivity, misfit_rows = (
        lax.all_to_all(columns, "chan", split_axis=0, concat_axis=1, tiled=True),
        lax.all_to_all(jacobian, "chan", split_axis=0, concat_axis=1, tiled=True),
        lax.all_to_all(
            innovation.astype(jnp.bfloat16), "chan", split_axis=0, concat_axis=1, tiled=True
        ).astype(innovation.dtype),
    )
    response = jnp.einsum("fcl,flk->fck", sensitivity, columns, preferred_element_type=jnp.float32)
    row_weights = lax.dynamic_slice_in_dim(
        live_rows, lax.axis_index("chan") * share_rows, share_rows, 0
    )
    scales = 1.0 / jnp.sqrt(error_values)
    whitened = (
        turn_blocks(response, error_vectors) * scales[None, :, None] * row_weights[:, None, None]
    )
    misfit = turn_rows(misfit_rows, error_vectors) * scales[None, :]
    pull_sum = jnp.einsum("fck,fc->k", whitened, misfit, precision=lax.Precision.HIGHEST)
    rounded = whitened.astype(jnp.bfloat16).reshape(-1, members)
    gram_sum = lax.dot_general(
        rounded, rounded, (((0,), (0,)), ((), ())), preferred_element_type=jnp.float32
    )
    return gram_sum, pull_sum


def local(
    ensemble,
    jacobian,
    innovation,
    error_vectors,
    error_values,
    ensemble_vectors,
    column_pick,
    footprint_slot,
    footprint_count,
):
    members = ensemble.shape[2]
    route = exchange if fits(ensemble, jacobian, column_pick, footprint_slot) else exchange_plain
    gram_sum, pull_sum = route(
        ensemble, jacobian, innovation, error_vectors, error_values, column_pick, footprint_slot, footprint_count
    )
    sums = sum_all(gram_sum, pull_sum)
    updated = finish(sums, ensemble_vectors, ensemble.reshape(-1, members))
    return updated.reshape(ensemble.shape)


def solution(mesh):
    return jax.shard_map(
        local,
        mesh=mesh,
        in_specs=(
            P("tile", "chan", None),
            P("tile", "chan", None),
            P("tile", "chan"),
            P(),
            P(),
            P(),
            P("tile", None, None),
            P("tile"),
            P("tile"),
        ),
        out_specs=P("tile", "chan", None),
        check_vma=False,
    )
```

```python
import functools
import jax
import jax.numpy as jnp
from jax import lax
from jax.experimental import pallas as pl
from jax.experimental.pallas import tpu as pltpu
from jax.sharding import PartitionSpec as P

MESH = pl.DeviceIdType.MESH


def greet(axes):
    barrier = pltpu.get_barrier_semaphore()
    total = 0
    for axis in axes:
        count = lax.axis_size(axis)
        here = lax.axis_index(axis)
        for step in range(1, count):
            pl.semaphore_signal(
                barrier, inc=1, device_id={axis: lax.rem(here + step, count)}, device_id_type=MESH
            )
        total += count - 1
    pl.semaphore_wait(barrier, total)


def sum_kernel(piece, x_ref, out_ref, landed, crossed, mine, summed, spread, sems_a, sems_b, sems_c):
    tiles = lax.axis_size("tile")
    chans = lax.axis_size("chan")
    tile = lax.axis_index("tile")
    chan = lax.axis_index("chan")

    def rows_of(index):
        return pl.ds(pl.multiple_of(index * piece, 8), piece)

    copies = []
    for step in range(1, tiles):
        peer = lax.rem(tile + step, tiles)
        copies.append(
            pltpu.make_async_remote_copy(
                src_ref=x_ref.at[rows_of(peer)],
                dst_ref=landed.at[step],
                send_sem=sems_a.at[0, step],
                recv_sem=sems_a.at[1, step],
                device_id={"tile": peer},
                device_id_type=MESH,
            )
        )
    for copy in copies:
        copy.start()
    total = x_ref[rows_of(tile), :]
    for step, copy in enumerate(copies, 1):
        copy.wait_recv()
        total = total + landed[step]
    mine[...] = total
    crossings = []
    for step in range(1, chans):
        crossings.append(
            pltpu.make_async_remote_copy(
                src_ref=mine,
                dst_ref=crossed.at[step],
                send_sem=sems_b.at[0, step],
                recv_sem=sems_b.at[1, step],
                device_id={"chan": lax.rem(chan + step, chans)},
                device_id_type=MESH,
            )
        )
    for copy in crossings:
        copy.start()
    for step, copy in enumerate(crossings, 1):
        copy.wait_recv()
        total = total + crossed[step]
    summed[...] = total
    shares = []
    for step in range(1, tiles):
        shares.append(
            pltpu.make_async_remote_copy(
                src_ref=summed,
                dst_ref=spread.at[step],
                send_sem=sems_c.at[0, step],
                recv_sem=sems_c.at[1, step],
                device_id={"tile": lax.rem(tile + step, tiles)},
                device_id_type=MESH,
            )
        )
    for copy in shares:
        copy.start()
    out_ref[rows_of(tile), :] = total
    for step, copy in enumerate(shares, 1):
        copy.wait_recv()
        out_ref[rows_of(lax.rem(tile - step + tiles, tiles)), :] = spread[step]
    for copy in copies + crossings + shares:
        copy.wait_send()


def sum_kernel_alone(piece, *refs):
    greet(("tile", "chan"))
    sum_kernel(piece, *refs)


def sum_scratch(tiles, chans, piece, half):
    return [
        pltpu.VMEM((tiles, piece, half), jnp.float32),
        pltpu.VMEM((chans, piece, half), jnp.float32),
        pltpu.VMEM((piece, half), jnp.float32),
        pltpu.VMEM((piece, half), jnp.float32),
        pltpu.VMEM((tiles, piece, half), jnp.float32),
        pltpu.SemaphoreType.DMA((2, tiles)),
        pltpu.SemaphoreType.DMA((2, chans)),
        pltpu.SemaphoreType.DMA((2, tiles)),
    ]


def piece_rows(tiles, half):
    return -(-(3 * half + 8) // (8 * tiles)) * 8


def sum_all(gram, pull):
    tiles = lax.axis_size("tile")
    chans = lax.axis_size("chan")
    members = gram.shape[0]
    half = members // 2
    piece = piece_rows(tiles, half)
    flat = jnp.concatenate(
        [
            gram[:half, :half],
            gram[:half, half:],
            gram[half:, half:],
            pull.reshape(2, half),
            jnp.zeros((piece * tiles - 3 * half - 2, half), jnp.float32),
        ],
        0,
    )
    return pl.pallas_call(
        functools.partial(sum_kernel_alone, piece),
        out_shape=jax.ShapeDtypeStruct(flat.shape, jnp.float32),
        in_specs=[pl.BlockSpec(memory_space=pltpu.VMEM)],
        out_specs=pl.BlockSpec(memory_space=pltpu.VMEM),
        scratch_shapes=sum_scratch(tiles, chans, piece, half),
        compiler_params=pltpu.CompilerParams(collective_id=0, has_side_effects=True),
        name="sum_all",
    )(flat)


def invert_factor(d_ref, y_ref):
    size = d_ref.shape[0]
    step = 8
    shape = d_ref.shape
    y_ref[...] = (
        lax.broadcasted_iota(jnp.int32, shape, 0) == lax.broadcasted_iota(jnp.int32, shape, 1)
    ).astype(jnp.float32)
    for start in range(0, size, step):
        below = d_ref[start:, :]
        right = y_ref[start:, :]
        line = lax.broadcasted_iota(jnp.int32, below.shape, 0)
        columns = [
            jnp.broadcast_to(below[:, start + j : start + j + 1], below.shape) for j in range(step)
        ]
        rows = [below[j : j + 1, :] for j in range(step)]
        others = [right[j : j + 1, :] for j in range(step)]
        for j in range(step):
            pivot = columns[j][j : j + 1, :]
            inverse = 1.0 / pivot
            under = jnp.where(line > j, columns[j], 0.0)
            row = rows[j] * inverse
            other = others[j] * inverse
            for k in range(j + 1, step):
                entry = columns[j][k : k + 1, :]
                columns[k] = columns[k] - under * (columns[k][j : j + 1, :] * inverse)
                rows[k] = rows[k] - entry * row
                others[k] = others[k] - entry * other
            below = below - under * row
            right = right - under * other
            y_ref[start + j : start + j + 1, :] = others[j] * (1.0 / jnp.sqrt(pivot))
        if start + step < size:
            d_ref[start + step :, :] = below[step:, :]
            y_ref[start + step :, :] = right[step:, :]


def finish_kernel(pieces, sum_ref, vec_ref, ens_ref, out_ref, d_ref, first, second, ens_v, out_v, load_sem, sems):
    half = d_ref.shape[0]
    members = 2 * half
    load = pltpu.make_async_copy(ens_ref, ens_v, load_sem)
    load.start()
    dims = lambda a, b: (((a,), (b,)), ((), ()))

    def dot(x, y, a=1, b=0):
        return lax.dot_general(
            x, y, dims(a, b), precision=lax.Precision.HIGHEST, preferred_element_type=jnp.float32
        )

    eye = (
        lax.broadcasted_iota(jnp.int32, (half, half), 0) == lax.broadcasted_iota(jnp.int32, (half, half), 1)
    ).astype(jnp.float32) * (members - 1)
    d_ref[...] = sum_ref[:half, :] + eye
    invert_factor(d_ref, first)
    across = dot(first[...], sum_ref[half : 2 * half, :])
    d_ref[...] = sum_ref[2 * half : 3 * half, :] + eye - dot(across, across, 0, 0)
    invert_factor(d_ref, second)
    low = -dot(second[...], dot(across, first[...], 0, 0))
    pull = sum_ref[3 * half : 3 * half + 8, :]
    top_half = jnp.sum(first[...] * pull[0:1, :], axis=1, keepdims=True)
    low_half = jnp.sum(low * pull[0:1, :] + second[...] * pull[1:2, :], axis=1, keepdims=True)
    scale = float(members - 1) ** 0.5
    top_right = scale * vec_ref[:half, :] + top_half
    low_right = scale * vec_ref[half:, :] + low_half
    transform = jnp.concatenate(
        [dot(first[...], top_right, 0, 0) + dot(low, low_right, 0, 0), dot(second[...], low_right, 0, 0)], 0
    ).astype(jnp.bfloat16)
    load.wait()
    size = ens_ref.shape[0] // pieces
    writes = []
    for i in range(pieces):
        span = pl.ds(i * size, size)
        out_v[span, :] = jnp.dot(
            ens_v[span, :], transform, preferred_element_type=jnp.float32
        ).astype(jnp.bfloat16)
        writes.append(pltpu.make_async_copy(out_v.at[span], out_ref.at[span], sems.at[i]))
        writes[-1].start()
    for write in writes:
        write.wait()


def finish(sums, ensemble_vectors, rows):
    members = ensemble_vectors.shape[0]
    half = members // 2
    pieces = 8
    vmem = pl.BlockSpec(memory_space=pltpu.VMEM)
    return pl.pallas_call(
        functools.partial(finish_kernel, pieces),
        out_shape=jax.ShapeDtypeStruct(rows.shape, rows.dtype),
        in_specs=[vmem, vmem, pl.BlockSpec(memory_space=pltpu.HBM)],
        out_specs=pl.BlockSpec(memory_space=pltpu.HBM),
        scratch_shapes=[
            pltpu.VMEM((half, half), jnp.float32),
            pltpu.VMEM((half, half), jnp.float32),
            pltpu.VMEM((half, half), jnp.float32),
            pltpu.VMEM(rows.shape, rows.dtype),
            pltpu.VMEM(rows.shape, rows.dtype),
            pltpu.SemaphoreType.DMA,
            pltpu.SemaphoreType.DMA((pieces,)),
        ],
        compiler_params=pltpu.CompilerParams(vmem_limit_bytes=40 * 1024 * 1024),
        name="finish",
    )(sums, ensemble_vectors, rows)


def exchange_kernel(
    window, cap, chunks, share, piece,
    pick_ref, order_ref, slot_ref, live_ref, ens_ref, jac_ref, innov_ref, vec_ref, val_ref,
    sums_ref,
    gram_ref, pull_ref, parts_ref, basis_ref, high_ref, low_ref, innov_v, misfit_ref,
    ens_v, jac_s, jac_land, mis_land, mis_all, chosen, arr, col_s, col_land, white,
    ens_sem, sems_t, sems_j, sems_m, sems_c, *sum_refs,
):
    chans = lax.axis_size("chan")
    tiles = lax.axis_size("tile")
    tile = lax.axis_index("tile")
    chan = lax.axis_index("chan")
    reach = window // 2
    level_part, members = ens_ref.shape[1], ens_ref.shape[2]
    part, levels = jac_ref.shape[1], jac_ref.shape[2]
    rows = chunks * share
    load = pltpu.make_async_copy(ens_ref, ens_v, ens_sem)
    load.start()

    def chan_peer(step):
        return lax.rem(chan + step, chans)

    def tile_peer(slot):
        return lax.rem(tile + slot - reach + tiles, tiles)

    barrier = pltpu.get_barrier_semaphore()
    for step in range(1, chans):
        pl.semaphore_signal(barrier, inc=1, device_id={"chan": chan_peer(step)}, device_id_type=MESH)
    for step in range(1, tiles):
        pl.semaphore_signal(
            barrier, inc=1, device_id={"tile": lax.rem(tile + step, tiles)}, device_id_type=MESH
        )

    jac_copies, mis_copies = [], []
    for step in range(1, chans):
        peer = chan_peer(step)

        def take_jac(i, carry, peer=peer):
            jac_s[peer, i] = jac_ref[order_ref[peer * rows + i]]
            return carry

        lax.fori_loop(0, rows, take_jac, 0)
        jac_copies.append(pltpu.make_async_remote_copy(
            src_ref=jac_s.at[peer], dst_ref=jac_land.at[chan],
            send_sem=sems_j.at[0, step], recv_sem=sems_j.at[1, step],
            device_id={"chan": peer}, device_id_type=MESH))
        mis_copies.append(pltpu.make_async_remote_copy(
            src_ref=misfit_ref.at[peer], dst_ref=mis_land.at[chan],
            send_sem=sems_m.at[0, step], recv_sem=sems_m.at[1, step],
            device_id={"chan": peer}, device_id_type=MESH))

    def own_jac(i, carry):
        jac_land[chan, i] = jac_ref[order_ref[chan * rows + i]]
        return carry

    lax.fori_loop(0, rows, own_jac, 0)
    pl.semaphore_wait(barrier, chans - 1 + tiles - 1)
    for copy in jac_copies:
        copy.start()

    load.wait()
    offsets = sorted((s for s in range(window) if s != reach), key=lambda s: abs(s - reach))
    tile_copies = {}
    waiting = None
    for slot in offsets:
        def take_col(i, carry, slot=slot):
            chosen[slot, i] = ens_v[pick_ref[0, slot, i]]
            return carry

        lax.fori_loop(0, cap, take_col, 0)
        if waiting is not None:
            waiting.start()
        waiting = tile_copies[slot] = pltpu.make_async_remote_copy(
            src_ref=chosen.at[slot], dst_ref=arr[slot],
            send_sem=sems_t.at[0, slot], recv_sem=sems_t.at[1, slot],
            device_id={"tile": tile_peer(slot)}, device_id_type=MESH)

    def own_col(i, carry):
        arr[reach][i] = ens_v[pick_ref[0, reach, i]]
        return carry

    lax.fori_loop(0, cap, own_col, 0)
    waiting.start()

    landed = {reach}
    col_copies = {}

    def send_chunk(q):
        for slot in (q, q + 1):
            if slot not in landed:
                tile_copies[slot].wait_recv()
                landed.add(slot)

        def pick(peer, i):
            index = slot_ref[peer * rows + q * share + i] - q * cap
            near = arr[q][jnp.clip(index, 0, cap - 1)]
            far = arr[q + 1][jnp.clip(index - cap, 0, cap - 1)]
            return lax.select(index < cap, near, far)

        waiting = None
        for step in range(1, chans):
            peer = chan_peer(step)

            def take(i, carry, peer=peer):
                col_s[peer, q, i] = pick(peer, i)
                return carry

            lax.fori_loop(0, share, take, 0)
            if waiting is not None:
                waiting.start()
            waiting = col_copies[q, step] = pltpu.make_async_remote_copy(
                src_ref=col_s.at[peer, q], dst_ref=col_land.at[chan, q],
                send_sem=sems_c.at[0, q, step], recv_sem=sems_c.at[1, q, step],
                device_id={"chan": peer}, device_id_type=MESH)

        def own(i, carry):
            col_land[chan, q, i] = pick(chan, i)
            return carry

        lax.fori_loop(0, share, own, 0)
        waiting.start()

    channels = chans * part
    group = vec_ref.shape[1]
    shape = (channels, channels)
    same = (
        lax.broadcasted_iota(jnp.int32, shape, 0) // group == lax.broadcasted_iota(jnp.int32, shape, 1) // group
    )
    tiled = jnp.concatenate([vec_ref[...]] * (channels // group), 1)
    basis = jnp.where(same, tiled, 0.0) / jnp.sqrt(val_ref[...])
    basis_ref[...] = basis
    turned = basis.T
    high = turned.astype(jnp.bfloat16)
    high_ref[...] = high
    low_ref[...] = (turned - high.astype(jnp.float32)).astype(jnp.bfloat16)
    innov_v[...] = jnp.dot(
        innov_ref[...],
        basis_ref[pl.ds(pl.multiple_of(chan * part, 8), part), :],
        precision=lax.Precision.HIGHEST,
        preferred_element_type=jnp.float32,
    )

    def take_misfit(i, carry):
        for z in range(chans):
            misfit_ref[z, pl.ds(i, 1), :] = innov_v[pl.ds(order_ref[z * rows + i], 1), :]
        return carry

    lax.fori_loop(0, rows, take_misfit, 0)

    sequence = sorted(range(chunks), key=lambda q: max(abs(q - reach), abs(q + 1 - reach)))
    half = len(sequence) // 2
    for q in sequence[:half]:
        send_chunk(q)

    mis_land[chan] = misfit_ref[chan]
    for copy in mis_copies:
        copy.start()
    for copy in jac_copies + mis_copies:
        copy.wait_recv()
    total = mis_land[0]
    for z in range(1, chans):
        total = total + mis_land[z]
    mis_all[...] = total

    def whiten(i, carry):
        block = jac_land[:, i].reshape(chans * part, levels)
        turned = jnp.dot(high_ref[...], block, preferred_element_type=jnp.float32)
        turned = turned + jnp.dot(low_ref[...], block, preferred_element_type=jnp.float32)
        turned = turned * live_ref[chan * rows + i]
        first = turned.astype(jnp.bfloat16)
        white[i, :, :levels] = first
        white[i, :, levels:] = (turned - first.astype(jnp.float32)).astype(jnp.bfloat16)
        return carry

    lax.fori_loop(0, rows, whiten, 0)
    for q in sequence[half:]:
        send_chunk(q)

    gram_ref[...] = jnp.zeros_like(gram_ref)
    pull_ref[...] = jnp.zeros_like(pull_ref)
    pair = 2 if share % 2 == 0 else 1

    for q in sequence:
        for step in range(1, chans):
            col_copies[q, step].wait_recv()

        def add(i, carry, q=q):
            rounded, weights = [], []
            for k in range(pair):
                s = i * pair + k
                block = col_land[:, q, s].reshape(levels, members)
                both = jnp.concatenate([block, block], 0)
                rounded.append(
                    jnp.dot(white[q * share + s], both, preferred_element_type=jnp.float32).astype(jnp.bfloat16)
                )
                weights.append(mis_all[pl.ds(q * share + s, 1), :])
            rounded = jnp.concatenate(rounded, 0)
            weights = jnp.broadcast_to(jnp.concatenate(weights, 1), (8, pair * channels))
            first = weights.astype(jnp.bfloat16).astype(jnp.float32)
            line = lax.broadcasted_iota(jnp.int32, weights.shape, 0)
            left = jnp.where(line == 0, first, jnp.where(line == 1, weights - first, 0.0))
            pull_ref[...] += jnp.dot(left.astype(jnp.bfloat16), rounded, preferred_element_type=jnp.float32)
            gram_ref[...] += lax.dot_general(
                rounded, rounded, (((0,), (0,)), ((), ())), preferred_element_type=jnp.float32
            )
            return carry

        lax.fori_loop(0, share // pair, add, 0)
    for copy in mis_copies + jac_copies + list(tile_copies.values()) + list(col_copies.values()):
        copy.wait_send()
    half = members // 2
    parts_ref[:half, :] = gram_ref[:half, :half]
    parts_ref[half : 2 * half, :] = gram_ref[:half, half:]
    parts_ref[2 * half : 3 * half, :] = gram_ref[half:, half:]
    parts_ref[3 * half :, :] = jnp.zeros((parts_ref.shape[0] - 3 * half, half), jnp.float32)
    pull = pull_ref[0:1, :] + pull_ref[1:2, :]
    parts_ref[3 * half : 3 * half + 1, :] = pull[:, :half]
    parts_ref[3 * half + 1 : 3 * half + 2, :] = pull[:, half:]
    sum_kernel(piece, parts_ref, sums_ref, *sum_refs)


def fits(ensemble, jacobian, column_pick, footprint_slot):
    chans = lax.axis_size("chan")
    window, cap = column_pick.shape[1:]
    return (
        footprint_slot.shape[0] == (window - 1) * cap
        and cap % chans == 0
        and window <= lax.axis_size("tile")
        and ensemble.shape[1] % 16 == 0
        and jacobian.shape[1] % 16 == 0
        and ensemble.shape[1] * chans == jacobian.shape[2]
        and jacobian.shape[1] * chans == jacobian.shape[2]
        and jacobian.shape[2] % 128 == 0
    )


def exchange(ensemble, jacobian, innovation, error_vectors, error_values, column_pick, footprint_slot, footprint_count):
    chans = lax.axis_size("chan")
    chan = lax.axis_index("chan")
    window, cap = column_pick.shape[1:]
    foot_rows = footprint_slot.shape[0]
    chunks = window - 1
    share = cap // chans
    rows = chunks * share
    part, levels = jacobian.shape[1:]
    level_part, members = ensemble.shape[1:]
    channels = part * chans
    group = error_vectors.shape[1]
    rank = jnp.sum(footprint_slot[None, :] < footprint_slot[:, None], axis=1, dtype=jnp.int32)
    place = jnp.arange(foot_rows, dtype=jnp.int32)
    spot = place % rows
    wanted = (spot // share) * cap + (place // rows) * share + spot % share
    match = rank[None, :] == wanted[:, None]
    order = jnp.sum(jnp.where(match, place[None, :], 0), axis=1)
    slots = jnp.sum(jnp.where(match, footprint_slot[None, :], 0), axis=1)
    live = (order < footprint_count[0]).astype(jnp.float32)
    tiles = lax.axis_size("tile")
    piece = piece_rows(tiles, members // 2)
    sums = (piece * tiles, members // 2)
    vmem = pl.BlockSpec(memory_space=pltpu.VMEM)
    smem = pl.BlockSpec(memory_space=pltpu.SMEM)
    half = jnp.bfloat16
    return pl.pallas_call(
        functools.partial(exchange_kernel, window, cap, chunks, share, piece),
        out_shape=jax.ShapeDtypeStruct(sums, jnp.float32),
        in_specs=[smem] * 4 + [pl.BlockSpec(memory_space=pltpu.HBM)] + [vmem] * 4,
        out_specs=vmem,
        scratch_shapes=[
            pltpu.VMEM((members, members), jnp.float32),
            pltpu.VMEM((8, members), jnp.float32),
            pltpu.VMEM(sums, jnp.float32),
            pltpu.VMEM((channels, channels), jnp.float32),
            pltpu.VMEM((channels, channels), half),
            pltpu.VMEM((channels, channels), half),
            pltpu.VMEM((foot_rows, channels), jnp.float32),
            pltpu.VMEM((chans, rows, channels), jnp.float32),
            pltpu.VMEM(ensemble.shape, half),
            pltpu.VMEM((chans, rows, part, levels), half),
            pltpu.VMEM((chans, rows, part, levels), half),
            pltpu.VMEM((chans, rows, channels), jnp.float32),
            pltpu.VMEM((rows, channels), jnp.float32),
            pltpu.VMEM((window, cap, level_part, members), half),
            [pltpu.VMEM((cap, level_part, members), half) for _ in range(window)],
            pltpu.VMEM((chans, chunks, share, level_part, members), half),
            pltpu.VMEM((chans, chunks, share, level_part, members), half),
            pltpu.VMEM((rows, channels, 2 * levels), half),
            pltpu.SemaphoreType.DMA,
            pltpu.SemaphoreType.DMA((2, window)),
            pltpu.SemaphoreType.DMA((2, chans)),
            pltpu.SemaphoreType.DMA((2, chans)),
            pltpu.SemaphoreType.DMA((2, chunks, chans)),
            *sum_scratch(tiles, chans, piece, members // 2),
        ],
        compiler_params=pltpu.CompilerParams(
            collective_id=1, has_side_effects=True, vmem_limit_bytes=48 * 1024 * 1024
        ),
        name="exchange",
    )(column_pick, order, slots, live, ensemble, jacobian, innovation, error_vectors, error_values.reshape(1, -1))


def from_behind(value, axis, steps):
    count = lax.axis_size(axis)
    pairs = [(source, (source + steps) % count) for source in range(count)]
    return lax.ppermute(value, axis, pairs)


def turn_blocks(values, vectors):
    row_count, channels, members = values.shape
    group_width = vectors.shape[1]
    grouped = values.reshape(row_count, channels // group_width, group_width, members)
    basis_blocks = vectors.reshape(channels // group_width, group_width, group_width)
    turned = jnp.einsum("gce,fgck->fgek", basis_blocks, grouped, precision=lax.Precision.HIGHEST)
    return turned.reshape(row_count, channels, members)


def turn_rows(values, vectors):
    row_count, channels = values.shape
    group_width = vectors.shape[1]
    grouped = values.reshape(row_count, channels // group_width, group_width)
    basis_blocks = vectors.reshape(channels // group_width, group_width, group_width)
    turned = jnp.einsum("gce,fgc->fge", basis_blocks, grouped, precision=lax.Precision.HIGHEST)
    return turned.reshape(row_count, channels)


def exchange_plain(
    ensemble, jacobian, innovation, error_vectors, error_values, column_pick, footprint_slot, footprint_count
):
    window = column_pick.shape[1]
    capacity = column_pick.shape[2]
    reach_tiles = window // 2
    level_part = ensemble.shape[1]
    members = ensemble.shape[2]
    chosen = jnp.take(ensemble, column_pick[0].reshape(-1), axis=0).reshape(
        window, capacity, level_part, members
    )
    blocks = []
    for slot_index in range(window):
        shift_by = slot_index - reach_tiles
        if shift_by == 0:
            blocks.append(chosen[slot_index])
        else:
            blocks.append(from_behind(chosen[slot_index], "tile", shift_by))
    arrived = jnp.stack(blocks, 0)
    slot_rows = arrived.reshape(window * capacity, level_part, members)
    columns = jnp.take(slot_rows, footprint_slot, axis=0)
    foot_rows = columns.shape[0]
    live_rows = (jnp.arange(foot_rows, dtype=jnp.int32) < footprint_count[0]).astype(jnp.float32)
    share_rows = foot_rows // lax.axis_size("chan")
    columns, sensitivity, misfit_rows = (
        lax.all_to_all(columns, "chan", split_axis=0, concat_axis=1, tiled=True),
        lax.all_to_all(jacobian, "chan", split_axis=0, concat_axis=1, tiled=True),
        lax.all_to_all(
            innovation.astype(jnp.bfloat16), "chan", split_axis=0, concat_axis=1, tiled=True
        ).astype(innovation.dtype),
    )
    response = jnp.einsum("fcl,flk->fck", sensitivity, columns, preferred_element_type=jnp.float32)
    row_weights = lax.dynamic_slice_in_dim(
        live_rows, lax.axis_index("chan") * share_rows, share_rows, 0
    )
    scales = 1.0 / jnp.sqrt(error_values)
    whitened = (
        turn_blocks(response, error_vectors) * scales[None, :, None] * row_weights[:, None, None]
    )
    misfit = turn_rows(misfit_rows, error_vectors) * scales[None, :]
    pull_sum = jnp.einsum("fck,fc->k", whitened, misfit, precision=lax.Precision.HIGHEST)
    rounded = whitened.astype(jnp.bfloat16).reshape(-1, members)
    gram_sum = lax.dot_general(
        rounded, rounded, (((0,), (0,)), ((), ())), preferred_element_type=jnp.float32
    )
    return sum_all(gram_sum, pull_sum)


def local(
    ensemble,
    jacobian,
    innovation,
    error_vectors,
    error_values,
    ensemble_vectors,
    column_pick,
    footprint_slot,
    footprint_count,
):
    members = ensemble.shape[2]
    route = exchange if fits(ensemble, jacobian, column_pick, footprint_slot) else exchange_plain
    sums = route(
        ensemble, jacobian, innovation, error_vectors, error_values, column_pick, footprint_slot, footprint_count
    )
    updated = finish(sums, ensemble_vectors, ensemble.reshape(-1, members))
    return updated.reshape(ensemble.shape)


def solution(mesh):
    return jax.shard_map(
        local,
        mesh=mesh,
        in_specs=(
            P("tile", "chan", None),
            P("tile", "chan", None),
            P("tile", "chan"),
            P(),
            P(),
            P(),
            P("tile", None, None),
            P("tile"),
            P("tile"),
        ),
        out_specs=P("tile", "chan", None),
        check_vma=False,
    )
```

```python
import functools
import jax
import jax.numpy as jnp
from jax import lax
from jax.experimental import pallas as pl
from jax.experimental.pallas import tpu as pltpu
from jax.sharding import PartitionSpec as P

MESH = pl.DeviceIdType.MESH


def greet(axes):
    barrier = pltpu.get_barrier_semaphore()
    total = 0
    for axis in axes:
        count = lax.axis_size(axis)
        here = lax.axis_index(axis)
        for step in range(1, count):
            pl.semaphore_signal(
                barrier, inc=1, device_id={axis: lax.rem(here + step, count)}, device_id_type=MESH
            )
        total += count - 1
    pl.semaphore_wait(barrier, total)


def sum_kernel(piece, x_ref, out_ref, landed, crossed, mine, summed, spread, sems_a, sems_b, sems_c):
    tiles = lax.axis_size("tile")
    chans = lax.axis_size("chan")
    tile = lax.axis_index("tile")
    chan = lax.axis_index("chan")

    def rows_of(index):
        return pl.ds(pl.multiple_of(index * piece, 8), piece)

    copies = []
    for step in range(1, tiles):
        peer = lax.rem(tile + step, tiles)
        copies.append(
            pltpu.make_async_remote_copy(
                src_ref=x_ref.at[rows_of(peer)],
                dst_ref=landed.at[step],
                send_sem=sems_a.at[0, step],
                recv_sem=sems_a.at[1, step],
                device_id={"tile": peer},
                device_id_type=MESH,
            )
        )
    for copy in copies:
        copy.start()
    total = x_ref[rows_of(tile), :]
    for step, copy in enumerate(copies, 1):
        copy.wait_recv()
        total = total + landed[step]
    mine[...] = total
    crossings = []
    for step in range(1, chans):
        crossings.append(
            pltpu.make_async_remote_copy(
                src_ref=mine,
                dst_ref=crossed.at[step],
                send_sem=sems_b.at[0, step],
                recv_sem=sems_b.at[1, step],
                device_id={"chan": lax.rem(chan + step, chans)},
                device_id_type=MESH,
            )
        )
    for copy in crossings:
        copy.start()
    for step, copy in enumerate(crossings, 1):
        copy.wait_recv()
        total = total + crossed[step]
    summed[...] = total
    shares = []
    for step in range(1, tiles):
        shares.append(
            pltpu.make_async_remote_copy(
                src_ref=summed,
                dst_ref=spread.at[step],
                send_sem=sems_c.at[0, step],
                recv_sem=sems_c.at[1, step],
                device_id={"tile": lax.rem(tile + step, tiles)},
                device_id_type=MESH,
            )
        )
    for copy in shares:
        copy.start()
    out_ref[rows_of(tile), :] = total
    for step, copy in enumerate(shares, 1):
        copy.wait_recv()
        out_ref[rows_of(lax.rem(tile - step + tiles, tiles)), :] = spread[step]
    for copy in copies + crossings + shares:
        copy.wait_send()


def sum_kernel_alone(piece, *refs):
    greet(("tile", "chan"))
    sum_kernel(piece, *refs)


def sum_scratch(tiles, chans, piece, half):
    return [
        pltpu.VMEM((tiles, piece, half), jnp.float32),
        pltpu.VMEM((chans, piece, half), jnp.float32),
        pltpu.VMEM((piece, half), jnp.float32),
        pltpu.VMEM((piece, half), jnp.float32),
        pltpu.VMEM((tiles, piece, half), jnp.float32),
        pltpu.SemaphoreType.DMA((2, tiles)),
        pltpu.SemaphoreType.DMA((2, chans)),
        pltpu.SemaphoreType.DMA((2, tiles)),
    ]


def piece_rows(tiles, half):
    return -(-(3 * half + 8) // (8 * tiles)) * 8


def sum_all(gram, pull):
    tiles = lax.axis_size("tile")
    chans = lax.axis_size("chan")
    members = gram.shape[0]
    half = members // 2
    piece = piece_rows(tiles, half)
    flat = jnp.concatenate(
        [
            gram[:half, :half],
            gram[:half, half:],
            gram[half:, half:],
            pull.reshape(2, half),
            jnp.zeros((piece * tiles - 3 * half - 2, half), jnp.float32),
        ],
        0,
    )
    return pl.pallas_call(
        functools.partial(sum_kernel_alone, piece),
        out_shape=jax.ShapeDtypeStruct(flat.shape, jnp.float32),
        in_specs=[pl.BlockSpec(memory_space=pltpu.VMEM)],
        out_specs=pl.BlockSpec(memory_space=pltpu.VMEM),
        scratch_shapes=sum_scratch(tiles, chans, piece, half),
        compiler_params=pltpu.CompilerParams(collective_id=0, has_side_effects=True),
        name="sum_all",
    )(flat)


def invert_factor(d_ref, y_ref):
    size = d_ref.shape[0]
    step = 8
    shape = d_ref.shape
    y_ref[...] = (
        lax.broadcasted_iota(jnp.int32, shape, 0) == lax.broadcasted_iota(jnp.int32, shape, 1)
    ).astype(jnp.float32)
    for start in range(0, size, step):
        below = d_ref[start:, :]
        right = y_ref[start:, :]
        line = lax.broadcasted_iota(jnp.int32, below.shape, 0)
        columns = [
            jnp.broadcast_to(below[:, start + j : start + j + 1], below.shape) for j in range(step)
        ]
        rows = [below[j : j + 1, :] for j in range(step)]
        others = [right[j : j + 1, :] for j in range(step)]
        for j in range(step):
            pivot = columns[j][j : j + 1, :]
            inverse = 1.0 / pivot
            under = jnp.where(line > j, columns[j], 0.0)
            row = rows[j] * inverse
            other = others[j] * inverse
            for k in range(j + 1, step):
                entry = columns[j][k : k + 1, :]
                columns[k] = columns[k] - under * (columns[k][j : j + 1, :] * inverse)
                rows[k] = rows[k] - entry * row
                others[k] = others[k] - entry * other
            below = below - under * row
            right = right - under * other
            y_ref[start + j : start + j + 1, :] = others[j] * (1.0 / jnp.sqrt(pivot))
        if start + step < size:
            d_ref[start + step :, :] = below[step:, :]
            y_ref[start + step :, :] = right[step:, :]


def finish_kernel(pieces, sum_ref, vec_ref, ens_ref, out_ref, d_ref, first, second, ens_v, out_v, load_sem, sems):
    half = d_ref.shape[0]
    members = 2 * half
    load = pltpu.make_async_copy(ens_ref, ens_v, load_sem)
    load.start()
    dims = lambda a, b: (((a,), (b,)), ((), ()))

    def dot(x, y, a=1, b=0):
        return lax.dot_general(
            x, y, dims(a, b), precision=lax.Precision.HIGHEST, preferred_element_type=jnp.float32
        )

    eye = (
        lax.broadcasted_iota(jnp.int32, (half, half), 0) == lax.broadcasted_iota(jnp.int32, (half, half), 1)
    ).astype(jnp.float32) * (members - 1)
    d_ref[...] = sum_ref[:half, :] + eye
    invert_factor(d_ref, first)
    across = dot(first[...], sum_ref[half : 2 * half, :])
    d_ref[...] = sum_ref[2 * half : 3 * half, :] + eye - dot(across, across, 0, 0)
    invert_factor(d_ref, second)
    low = -dot(second[...], dot(across, first[...], 0, 0))
    pull = sum_ref[3 * half : 3 * half + 8, :]
    top_half = jnp.sum(first[...] * pull[0:1, :], axis=1, keepdims=True)
    low_half = jnp.sum(low * pull[0:1, :] + second[...] * pull[1:2, :], axis=1, keepdims=True)
    scale = float(members - 1) ** 0.5
    top_right = scale * vec_ref[:half, :] + top_half
    low_right = scale * vec_ref[half:, :] + low_half
    transform = jnp.concatenate(
        [dot(first[...], top_right, 0, 0) + dot(low, low_right, 0, 0), dot(second[...], low_right, 0, 0)], 0
    ).astype(jnp.bfloat16)
    load.wait()
    size = ens_ref.shape[0] // pieces
    writes = []
    for i in range(pieces):
        span = pl.ds(i * size, size)
        out_v[span, :] = jnp.dot(
            ens_v[span, :], transform, preferred_element_type=jnp.float32
        ).astype(jnp.bfloat16)
        writes.append(pltpu.make_async_copy(out_v.at[span], out_ref.at[span], sems.at[i]))
        writes[-1].start()
    for write in writes:
        write.wait()


def finish(sums, ensemble_vectors, rows):
    members = ensemble_vectors.shape[0]
    half = members // 2
    pieces = 8
    vmem = pl.BlockSpec(memory_space=pltpu.VMEM)
    return pl.pallas_call(
        functools.partial(finish_kernel, pieces),
        out_shape=jax.ShapeDtypeStruct(rows.shape, rows.dtype),
        in_specs=[vmem, vmem, pl.BlockSpec(memory_space=pltpu.HBM)],
        out_specs=pl.BlockSpec(memory_space=pltpu.HBM),
        scratch_shapes=[
            pltpu.VMEM((half, half), jnp.float32),
            pltpu.VMEM((half, half), jnp.float32),
            pltpu.VMEM((half, half), jnp.float32),
            pltpu.VMEM(rows.shape, rows.dtype),
            pltpu.VMEM(rows.shape, rows.dtype),
            pltpu.SemaphoreType.DMA,
            pltpu.SemaphoreType.DMA((pieces,)),
        ],
        compiler_params=pltpu.CompilerParams(vmem_limit_bytes=40 * 1024 * 1024),
        name="finish",
    )(sums, ensemble_vectors, rows)


def exchange_kernel(
    window, cap, chunks, share, piece,
    pick_ref, order_ref, slot_ref, live_ref, ens_ref, jac_ref, innov_ref, vec_ref, val_ref,
    sums_ref,
    gram_ref, pull_ref, parts_ref, basis_ref, high_ref, low_ref, innov_v, misfit_ref,
    ens_v, jac_s, jac_land, mis_land, mis_all, chosen, arr, col_s, col_land, white,
    ens_sem, sems_t, sems_j, sems_m, sems_c, *sum_refs,
):
    chans = lax.axis_size("chan")
    tiles = lax.axis_size("tile")
    tile = lax.axis_index("tile")
    chan = lax.axis_index("chan")
    reach = window // 2
    level_part, members = ens_ref.shape[1], ens_ref.shape[2]
    part, levels = jac_ref.shape[1], jac_ref.shape[2]
    rows = chunks * share
    load = pltpu.make_async_copy(ens_ref, ens_v, ens_sem)
    load.start()

    def chan_peer(step):
        return lax.rem(chan + step, chans)

    def tile_peer(slot):
        return lax.rem(tile + slot - reach + tiles, tiles)

    barrier = pltpu.get_barrier_semaphore()
    for step in range(1, chans):
        pl.semaphore_signal(barrier, inc=1, device_id={"chan": chan_peer(step)}, device_id_type=MESH)
    for step in range(1, tiles):
        pl.semaphore_signal(
            barrier, inc=1, device_id={"tile": lax.rem(tile + step, tiles)}, device_id_type=MESH
        )

    jac_copies, mis_copies = [], []
    for step in range(1, chans):
        peer = chan_peer(step)

        def take_jac(i, carry, peer=peer):
            jac_s[peer, i] = jac_ref[order_ref[peer * rows + i]]
            return carry

        lax.fori_loop(0, rows, take_jac, 0)
        jac_copies.append(pltpu.make_async_remote_copy(
            src_ref=jac_s.at[peer], dst_ref=jac_land.at[chan],
            send_sem=sems_j.at[0, step], recv_sem=sems_j.at[1, step],
            device_id={"chan": peer}, device_id_type=MESH))
        mis_copies.append(pltpu.make_async_remote_copy(
            src_ref=misfit_ref.at[peer], dst_ref=mis_land.at[chan],
            send_sem=sems_m.at[0, step], recv_sem=sems_m.at[1, step],
            device_id={"chan": peer}, device_id_type=MESH))

    def own_jac(i, carry):
        jac_land[chan, i] = jac_ref[order_ref[chan * rows + i]]
        return carry

    lax.fori_loop(0, rows, own_jac, 0)
    pl.semaphore_wait(barrier, chans - 1 + tiles - 1)
    for copy in jac_copies:
        copy.start()

    load.wait()
    offsets = sorted((s for s in range(window) if s != reach), key=lambda s: abs(s - reach))
    tile_copies = {}
    waiting = None
    for slot in offsets:
        def take_col(i, carry, slot=slot):
            chosen[slot, i] = ens_v[pick_ref[0, slot, i]]
            return carry

        lax.fori_loop(0, cap, take_col, 0)
        if waiting is not None:
            waiting.start()
        waiting = tile_copies[slot] = pltpu.make_async_remote_copy(
            src_ref=chosen.at[slot], dst_ref=arr[slot],
            send_sem=sems_t.at[0, slot], recv_sem=sems_t.at[1, slot],
            device_id={"tile": tile_peer(slot)}, device_id_type=MESH)

    def own_col(i, carry):
        arr[reach][i] = ens_v[pick_ref[0, reach, i]]
        return carry

    lax.fori_loop(0, cap, own_col, 0)
    waiting.start()

    landed = {reach}
    col_copies = {}

    def send_chunk(q):
        for slot in (q, q + 1):
            if slot not in landed:
                tile_copies[slot].wait_recv()
                landed.add(slot)

        def pick(peer, i):
            index = slot_ref[peer * rows + q * share + i] - q * cap
            near = arr[q][jnp.clip(index, 0, cap - 1)]
            far = arr[q + 1][jnp.clip(index - cap, 0, cap - 1)]
            return lax.select(index < cap, near, far)

        waiting = None
        for step in range(1, chans):
            peer = chan_peer(step)

            def take(i, carry, peer=peer):
                col_s[peer, q, i] = pick(peer, i)
                return carry

            lax.fori_loop(0, share, take, 0)
            if waiting is not None:
                waiting.start()
            waiting = col_copies[q, step] = pltpu.make_async_remote_copy(
                src_ref=col_s.at[peer, q], dst_ref=col_land.at[chan, q],
                send_sem=sems_c.at[0, q, step], recv_sem=sems_c.at[1, q, step],
                device_id={"chan": peer}, device_id_type=MESH)

        def own(i, carry):
            col_land[chan, q, i] = pick(chan, i)
            return carry

        lax.fori_loop(0, share, own, 0)
        waiting.start()

    channels = chans * part
    group = vec_ref.shape[0]
    shape = (channels, channels)
    same = (
        lax.broadcasted_iota(jnp.int32, shape, 0) // group == lax.broadcasted_iota(jnp.int32, shape, 1) // group
    )
    tiled = jnp.concatenate([vec_ref[...]] * (channels // group), 0).T
    basis = jnp.where(same, tiled, 0.0) / jnp.sqrt(val_ref[...])
    basis_ref[...] = basis
    turned = basis.T
    high = turned.astype(jnp.bfloat16)
    high_ref[...] = high
    low_ref[...] = (turned - high.astype(jnp.float32)).astype(jnp.bfloat16)
    innov_v[...] = lax.dot_general(
        innov_ref[...],
        basis_ref[pl.ds(pl.multiple_of(chan * part, 8), part), :],
        (((0,), (0,)), ((), ())),
        precision=lax.Precision.HIGHEST,
        preferred_element_type=jnp.float32,
    )

    def take_misfit(i, carry):
        for z in range(chans):
            misfit_ref[z, pl.ds(i, 1), :] = innov_v[pl.ds(order_ref[z * rows + i], 1), :]
        return carry

    lax.fori_loop(0, rows, take_misfit, 0)
    mis_land[chan] = misfit_ref[chan]
    for copy in mis_copies:
        copy.start()

    sequence = sorted(range(chunks), key=lambda q: max(abs(q - reach), abs(q + 1 - reach)))
    half = len(sequence) // 2
    for q in sequence[:half]:
        send_chunk(q)

    for copy in jac_copies:
        copy.wait_recv()

    def whiten(i, carry):
        block = jac_land[:, i].reshape(chans * part, levels)
        turned = jnp.dot(high_ref[...], block, preferred_element_type=jnp.float32)
        turned = turned + jnp.dot(low_ref[...], block, preferred_element_type=jnp.float32)
        turned = turned * live_ref[chan * rows + i]
        first = turned.astype(jnp.bfloat16)
        white[i, :, :levels] = first
        white[i, :, levels:] = (turned - first.astype(jnp.float32)).astype(jnp.bfloat16)
        return carry

    lax.fori_loop(0, rows, whiten, 0)
    for q in sequence[half:]:
        send_chunk(q)
    for copy in mis_copies:
        copy.wait_recv()
    total = mis_land[0]
    for z in range(1, chans):
        total = total + mis_land[z]
    mis_all[...] = total

    gram_ref[...] = jnp.zeros_like(gram_ref)
    pull_ref[...] = jnp.zeros_like(pull_ref)
    pair = 2 if share % 2 == 0 else 1

    for q in sequence:
        for step in range(1, chans):
            col_copies[q, step].wait_recv()

        def add(i, carry, q=q):
            rounded, weights = [], []
            for k in range(pair):
                s = i * pair + k
                block = col_land[:, q, s].reshape(levels, members)
                both = jnp.concatenate([block, block], 0)
                rounded.append(
                    jnp.dot(white[q * share + s], both, preferred_element_type=jnp.float32).astype(jnp.bfloat16)
                )
                weights.append(mis_all[pl.ds(q * share + s, 1), :])
            rounded = jnp.concatenate(rounded, 0)
            weights = jnp.broadcast_to(jnp.concatenate(weights, 1), (8, pair * channels))
            first = weights.astype(jnp.bfloat16).astype(jnp.float32)
            line = lax.broadcasted_iota(jnp.int32, weights.shape, 0)
            left = jnp.where(line == 0, first, jnp.where(line == 1, weights - first, 0.0))
            pull_ref[...] += jnp.dot(left.astype(jnp.bfloat16), rounded, preferred_element_type=jnp.float32)
            gram_ref[...] += lax.dot_general(
                rounded, rounded, (((0,), (0,)), ((), ())), preferred_element_type=jnp.float32
            )
            return carry

        lax.fori_loop(0, share // pair, add, 0)
    for copy in mis_copies + jac_copies + list(tile_copies.values()) + list(col_copies.values()):
        copy.wait_send()
    half = members // 2
    parts_ref[:half, :] = gram_ref[:half, :half]
    parts_ref[half : 2 * half, :] = gram_ref[:half, half:]
    parts_ref[2 * half : 3 * half, :] = gram_ref[half:, half:]
    parts_ref[3 * half :, :] = jnp.zeros((parts_ref.shape[0] - 3 * half, half), jnp.float32)
    pull = pull_ref[0:1, :] + pull_ref[1:2, :]
    parts_ref[3 * half : 3 * half + 1, :] = pull[:, :half]
    parts_ref[3 * half + 1 : 3 * half + 2, :] = pull[:, half:]
    sum_kernel(piece, parts_ref, sums_ref, *sum_refs)


def fits(ensemble, jacobian, column_pick, footprint_slot):
    chans = lax.axis_size("chan")
    window, cap = column_pick.shape[1:]
    return (
        footprint_slot.shape[0] == (window - 1) * cap
        and cap % chans == 0
        and window <= lax.axis_size("tile")
        and ensemble.shape[1] % 16 == 0
        and jacobian.shape[1] % 16 == 0
        and ensemble.shape[1] * chans == jacobian.shape[2]
        and jacobian.shape[1] * chans == jacobian.shape[2]
        and jacobian.shape[2] % 128 == 0
    )


def exchange(ensemble, jacobian, innovation, error_vectors, error_values, column_pick, footprint_slot, footprint_count):
    chans = lax.axis_size("chan")
    chan = lax.axis_index("chan")
    window, cap = column_pick.shape[1:]
    foot_rows = footprint_slot.shape[0]
    chunks = window - 1
    share = cap // chans
    rows = chunks * share
    part, levels = jacobian.shape[1:]
    level_part, members = ensemble.shape[1:]
    channels = part * chans
    group = error_vectors.shape[1]
    rank = jnp.sum(footprint_slot[None, :] < footprint_slot[:, None], axis=1, dtype=jnp.int32)
    place = jnp.arange(foot_rows, dtype=jnp.int32)
    spot = place % rows
    wanted = (spot // share) * cap + (place // rows) * share + spot % share
    match = rank[None, :] == wanted[:, None]
    order = jnp.sum(jnp.where(match, place[None, :], 0), axis=1)
    slots = jnp.sum(jnp.where(match, footprint_slot[None, :], 0), axis=1)
    live = (order < footprint_count[0]).astype(jnp.float32)
    tiles = lax.axis_size("tile")
    piece = piece_rows(tiles, members // 2)
    sums = (piece * tiles, members // 2)
    vmem = pl.BlockSpec(memory_space=pltpu.VMEM)
    smem = pl.BlockSpec(memory_space=pltpu.SMEM)
    half = jnp.bfloat16
    return pl.pallas_call(
        functools.partial(exchange_kernel, window, cap, chunks, share, piece),
        out_shape=jax.ShapeDtypeStruct(sums, jnp.float32),
        in_specs=[smem] * 4 + [pl.BlockSpec(memory_space=pltpu.HBM)] + [vmem] * 4,
        out_specs=vmem,
        scratch_shapes=[
            pltpu.VMEM((members, members), jnp.float32),
            pltpu.VMEM((8, members), jnp.float32),
            pltpu.VMEM(sums, jnp.float32),
            pltpu.VMEM((channels, channels), jnp.float32),
            pltpu.VMEM((channels, channels), half),
            pltpu.VMEM((channels, channels), half),
            pltpu.VMEM((foot_rows, channels), jnp.float32),
            pltpu.VMEM((chans, rows, channels), jnp.float32),
            pltpu.VMEM(ensemble.shape, half),
            pltpu.VMEM((chans, rows, part, levels), half),
            pltpu.VMEM((chans, rows, part, levels), half),
            pltpu.VMEM((chans, rows, channels), jnp.float32),
            pltpu.VMEM((rows, channels), jnp.float32),
            pltpu.VMEM((window, cap, level_part, members), half),
            [pltpu.VMEM((cap, level_part, members), half) for _ in range(window)],
            pltpu.VMEM((chans, chunks, share, level_part, members), half),
            pltpu.VMEM((chans, chunks, share, level_part, members), half),
            pltpu.VMEM((rows, channels, 2 * levels), half),
            pltpu.SemaphoreType.DMA,
            pltpu.SemaphoreType.DMA((2, window)),
            pltpu.SemaphoreType.DMA((2, chans)),
            pltpu.SemaphoreType.DMA((2, chans)),
            pltpu.SemaphoreType.DMA((2, chunks, chans)),
            *sum_scratch(tiles, chans, piece, members // 2),
        ],
        compiler_params=pltpu.CompilerParams(
            collective_id=1, has_side_effects=True, vmem_limit_bytes=48 * 1024 * 1024
        ),
        name="exchange",
    )(column_pick, order, slots, live, ensemble, jacobian, innovation.T, error_vectors.T, error_values.reshape(1, -1))


def from_behind(value, axis, steps):
    count = lax.axis_size(axis)
    pairs = [(source, (source + steps) % count) for source in range(count)]
    return lax.ppermute(value, axis, pairs)


def turn_blocks(values, vectors):
    row_count, channels, members = values.shape
    group_width = vectors.shape[1]
    grouped = values.reshape(row_count, channels // group_width, group_width, members)
    basis_blocks = vectors.reshape(channels // group_width, group_width, group_width)
    turned = jnp.einsum("gce,fgck->fgek", basis_blocks, grouped, precision=lax.Precision.HIGHEST)
    return turned.reshape(row_count, channels, members)


def turn_rows(values, vectors):
    row_count, channels = values.shape
    group_width = vectors.shape[1]
    grouped = values.reshape(row_count, channels // group_width, group_width)
    basis_blocks = vectors.reshape(channels // group_width, group_width, group_width)
    turned = jnp.einsum("gce,fgc->fge", basis_blocks, grouped, precision=lax.Precision.HIGHEST)
    return turned.reshape(row_count, channels)


def exchange_plain(
    ensemble, jacobian, innovation, error_vectors, error_values, column_pick, footprint_slot, footprint_count
):
    window = column_pick.shape[1]
    capacity = column_pick.shape[2]
    reach_tiles = window // 2
    level_part = ensemble.shape[1]
    members = ensemble.shape[2]
    chosen = jnp.take(ensemble, column_pick[0].reshape(-1), axis=0).reshape(
        window, capacity, level_part, members
    )
    blocks = []
    for slot_index in range(window):
        shift_by = slot_index - reach_tiles
        if shift_by == 0:
            blocks.append(chosen[slot_index])
        else:
            blocks.append(from_behind(chosen[slot_index], "tile", shift_by))
    arrived = jnp.stack(blocks, 0)
    slot_rows = arrived.reshape(window * capacity, level_part, members)
    columns = jnp.take(slot_rows, footprint_slot, axis=0)
    foot_rows = columns.shape[0]
    live_rows = (jnp.arange(foot_rows, dtype=jnp.int32) < footprint_count[0]).astype(jnp.float32)
    share_rows = foot_rows // lax.axis_size("chan")
    columns, sensitivity, misfit_rows = (
        lax.all_to_all(columns, "chan", split_axis=0, concat_axis=1, tiled=True),
        lax.all_to_all(jacobian, "chan", split_axis=0, concat_axis=1, tiled=True),
        lax.all_to_all(
            innovation.astype(jnp.bfloat16), "chan", split_axis=0, concat_axis=1, tiled=True
        ).astype(innovation.dtype),
    )
    response = jnp.einsum("fcl,flk->fck", sensitivity, columns, preferred_element_type=jnp.float32)
    row_weights = lax.dynamic_slice_in_dim(
        live_rows, lax.axis_index("chan") * share_rows, share_rows, 0
    )
    scales = 1.0 / jnp.sqrt(error_values)
    whitened = (
        turn_blocks(response, error_vectors) * scales[None, :, None] * row_weights[:, None, None]
    )
    misfit = turn_rows(misfit_rows, error_vectors) * scales[None, :]
    pull_sum = jnp.einsum("fck,fc->k", whitened, misfit, precision=lax.Precision.HIGHEST)
    rounded = whitened.astype(jnp.bfloat16).reshape(-1, members)
    gram_sum = lax.dot_general(
        rounded, rounded, (((0,), (0,)), ((), ())), preferred_element_type=jnp.float32
    )
    return sum_all(gram_sum, pull_sum)


def local(
    ensemble,
    jacobian,
    innovation,
    error_vectors,
    error_values,
    ensemble_vectors,
    column_pick,
    footprint_slot,
    footprint_count,
):
    members = ensemble.shape[2]
    route = exchange if fits(ensemble, jacobian, column_pick, footprint_slot) else exchange_plain
    sums = route(
        ensemble, jacobian, innovation, error_vectors, error_values, column_pick, footprint_slot, footprint_count
    )
    updated = finish(sums, ensemble_vectors, ensemble.reshape(-1, members))
    return updated.reshape(ensemble.shape)


def solution(mesh):
    return jax.shard_map(
        local,
        mesh=mesh,
        in_specs=(
            P("tile", "chan", None),
            P("tile", "chan", None),
            P("tile", "chan"),
            P(),
            P(),
            P(),
            P("tile", None, None),
            P("tile"),
            P("tile"),
        ),
        out_specs=P("tile", "chan", None),
        check_vma=False,
    )
```
